512 devices in a mesh: dp: 8 (over y), seq: 64 (over z, x, core).
Axes of the slice: x: 4, y: 8, z: 8, core: 2. Of those that a mesh axis runs over, the one named last changes fastest.
Arguments:
- queries: bfloat16 [8, 8192, 1536], P('dp', 'seq'), may hold values from -6 to 6
- keys: bfloat16 [8, 8192, 1536], P('dp', 'seq'), may hold values from -6 to 6
- values: bfloat16 [8, 8192, 1536], P('dp', 'seq'), may hold values from -6 to 6
- segment_ids: int32 [8, 8192], P('dp'), may hold values from 0 to 127, never falling along the last dimension, each value on 1 to 128 neighbouring positions
- norm_gain: float32 [1536], replicated, may hold values from 0.25 to 1.75
- conv_kernel: float32 [31, 1536], replicated, may hold values from -1 to 1
- conv_bias: float32 [1536], replicated, may hold values from -3 to 3
- cotangent: bfloat16 [8, 8192, 1536], P('dp', 'seq'), may hold values from -6 to 6
Outputs:
- conv_out: bfloat16 [8, 8192, 1536], P('dp', 'seq')
- query_grad: bfloat16 [8, 8192, 1536], P('dp', 'seq')
- key_grad: bfloat16 [8, 8192, 1536], P('dp', 'seq')
- value_grad: bfloat16 [8, 8192, 1536], P('dp', 'seq')
- gain_grad: float32 [1536], replicated
- kernel_grad: float32 [31, 1536], replicated
- bias_grad: float32 [1536], replicated
The draws below stay inside these ranges and needn't reach their ends.
Inputs may be any that keep to these rules, and one draw needn't show every extreme that they name: `segment_ids`: within each row, utterance numbers never fall; each utterance holds 1 to 128 frames, and some utterance exactly 128.
All inputs are finite; a program needn't handle non-finite values.
Results may differ from the reference program's by a relative error of at most 0.023.
Values may be sent and summed in bfloat16 or wider, within the bound.
A program may use at most 64 MiB of HBM per device.

```python
import math
import jax
import jax.numpy as jnp
import numpy as np
from jax import lax

HEADS = 24
HEAD_DIM = 64
D = 1536
KERNEL = 31
FRAMES_DEV = 128
MAX_LEN = 128
BATCH = 8
SEQLEN = 8192
SEGMENTS = 128


def paired_fields(key):
    base = jax.random.fold_in(key, 9173)
    first, second = jax.random.split(base, 2)
    shape = (BATCH, SEQLEN, HEADS, HEAD_DIM)
    query_part = jnp.clip(jax.random.normal(first, shape, jnp.float32), -6.0, 6.0)
    key_part = jnp.clip(jax.random.normal(second, shape, jnp.float32), -6.0, 6.0)
    return (query_part.reshape(BATCH, SEQLEN, HEADS * HEAD_DIM), key_part.reshape(BATCH, SEQLEN, HEADS * HEAD_DIM))


def draw_queries(key, part):
    return paired_fields(key)[0].astype(jnp.bfloat16)


def draw_keys(key, part):
    return paired_fields(key)[1].astype(jnp.bfloat16)


def steps_of(own_key, extent, pieces, smallest, high):
    def one(dim, parts):
        draws = jax.random.uniform(jax.random.fold_in(jax.random.fold_in(own_key, 6), dim), (parts,), jnp.float32, smallest / len(pieces), high / len(pieces))
        return jnp.repeat(jnp.exp(draws), extent[dim] // parts).reshape((-1,) + (1,) * (len(extent) - dim - 1))

    level = one(*pieces[0])
    for cut in pieces[1:]:
        level = level * one(*cut)
    return level


def length_profile(number_of, total, bound, skew):
    loads = [(1 << 20) // math.isqrt(rank ** skew) + 1 for rank in range(2, number_of + 1)]
    rest, counts = total - bound - (number_of - 1), [1] * (number_of - 1)
    while rest > 0:
        free = [i for i in range(number_of - 1) if counts[i] < bound]
        whole, budget = sum([loads[i] for i in free]), rest
        for i in free:
            extra = min(bound - counts[i], max(1, budget * loads[i] // whole), rest)
            counts[i] = counts[i] + extra
            rest = rest - extra
    return np.array([bound] + counts)


def ragged_sizes(own_key, amount, total, most, skew):
    if amount == 2:
        one = jax.random.randint(own_key, (), max(1, total - most), min(most, total - 1) + 1)
        return jnp.stack([one, total - one])
    sizes = jnp.asarray(length_profile(amount, total, most, skew), jnp.int32)
    couples = (amount - 1) // 2
    donor, taker = sizes[1:1 + 2 * couples:2], sizes[2:2 + 2 * couples:2]
    room = jnp.minimum(donor - 1, most - taker)
    moved = jax.random.randint(jax.random.fold_in(own_key, 1), (couples,), 0, 1 << 20) % (room + 1)
    sizes = sizes.at[1:1 + 2 * couples:2].set(donor - moved).at[2:2 + 2 * couples:2].set(taker + moved)
    return sizes[jax.random.permutation(jax.random.fold_in(own_key, 2), amount)]


def scatter_about(rng, extent, scale, most, shards=(), kind=jnp.bfloat16):
    drawn = scale * jax.random.normal(rng, extent, jnp.float32)
    if shards:
        drawn = drawn * steps_of(rng, extent, shards, -0.22, 0.18)
    return jnp.clip(drawn, -most, most).astype(kind)


def setup_inputs(seed: int = 0) -> dict:
    key_list = jax.random.split(jax.random.key(seed), 9)
    return {
        "queries": draw_queries(jax.random.fold_in(key_list[8], 71), 0),
        "keys": draw_keys(jax.random.fold_in(key_list[8], 71), 0),
        "values": scatter_about(key_list[2], (BATCH, SEQLEN, D), 1.0, 6.0, ((0, 8), (1, 64))),
        "segment_ids": jax.vmap(lambda own: jnp.searchsorted(jnp.cumsum(ragged_sizes(own, SEGMENTS, SEQLEN, MAX_LEN, 1)), jnp.arange(SEQLEN), side="right"))(jax.random.split(key_list[3], BATCH)).reshape((BATCH, SEQLEN)).astype(jnp.int32),
        "norm_gain": jnp.clip(1.0 + 0.15 * jax.random.normal(key_list[4], (D,), jnp.float32), 0.25, 1.75),
        "conv_kernel": scatter_about(key_list[5], (KERNEL, D), KERNEL ** -0.5, 1.0, (), jnp.float32),
        "conv_bias": scatter_about(key_list[6], (D,), 0.5, 3.0, (), jnp.float32),
        "cotangent": scatter_about(key_list[7], (BATCH, SEQLEN, D), 1.0, 6.0, ((0, 8), (1, 64))),
    }


EPS = 1e-05
NEG = -1e+30

def masked_logits(query_rows, key_rows, same_seg):
    factor = query_rows.shape[-1] ** (-0.5)
    logits = jnp.einsum('qhe,khe->hqk', query_rows.astype(jnp.float32), key_rows.astype(jnp.float32)) * factor
    return jnp.where(same_seg[None], logits, NEG)

def forward_block(query_rows, key_rows, value_rows, same_seg):
    logits = masked_logits(query_rows, key_rows, same_seg)
    row_top = lax.optimization_barrier(jnp.max(logits, -1, keepdims=True))
    exponent = jnp.exp(logits - row_top)
    row_total = lax.optimization_barrier(jnp.sum(exponent, -1, keepdims=True))
    attn_weights = (exponent / row_total).astype(jnp.bfloat16)
    context = jnp.einsum('hqk,khe->qhe', attn_weights.astype(jnp.float32), value_rows.astype(jnp.float32))
    return (context, (row_top + jnp.log(row_total))[..., 0])

def back_terms(query_rows, key_rows, value_rows, grad_rows, log_total, row_delta, same_seg):
    factor = query_rows.shape[-1] ** (-0.5)
    logits = masked_logits(query_rows, key_rows, same_seg)
    prob_back = jnp.exp(logits - log_total[:, :, None])
    grad_prob = jnp.einsum('qhe,khe->hqk', grad_rows.astype(jnp.float32), value_rows.astype(jnp.float32))
    grad_logit = (prob_back * (grad_prob - row_delta[:, :, None]) * factor).astype(jnp.bfloat16)
    return (prob_back.astype(jnp.bfloat16), grad_logit)

def row_pass(operands, norm_gain, conv_kernel, conv_bias):
    query_row, key_row, value_row, seg_row, cot_row = operands
    length = query_row.shape[0]
    width = query_row.shape[1]
    reach_rows = MAX_LEN
    frame_count = FRAMES_DEV
    half_taps = KERNEL // 2
    block_count = length // frame_count
    seg_row = seg_row.astype(jnp.int32)
    query_heads = query_row.reshape(length, HEADS, HEAD_DIM)
    key_heads = key_row.reshape(length, HEADS, HEAD_DIM)
    value_heads = value_row.reshape(length, HEADS, HEAD_DIM)
    edge_fill = jnp.full((reach_rows,), -1, jnp.int32)
    seg_padded = jnp.concatenate([edge_fill, seg_row, edge_fill])

    def pad_rows(tensor):
        return jnp.pad(tensor, ((reach_rows, reach_rows), (0, 0), (0, 0)))
    key_padded = pad_rows(key_heads)
    value_padded = pad_rows(value_heads)
    starts = jnp.arange(block_count, dtype=jnp.int32) * frame_count
    wide_count = frame_count + 2 * reach_rows

    def forward_one(start_row):
        own_seg = lax.dynamic_slice_in_dim(seg_row, start_row, frame_count)
        wide_seg = lax.dynamic_slice_in_dim(seg_padded, start_row, wide_count)
        return forward_block(lax.dynamic_slice_in_dim(query_heads, start_row, frame_count), lax.dynamic_slice_in_dim(key_padded, start_row, wide_count), lax.dynamic_slice_in_dim(value_padded, start_row, wide_count), own_seg[:, None] == wide_seg[None, :])
    context_blocks, total_blocks = lax.map(forward_one, starts)
    context = context_blocks.reshape(length, width).astype(jnp.bfloat16)
    total_rows = total_blocks.transpose(1, 0, 2).reshape(HEADS, length)
    context_f = context.astype(jnp.float32)
    row_mean = lax.optimization_barrier(jnp.mean(context_f, -1, keepdims=True))
    centred = context_f - row_mean
    inv_std = lax.rsqrt(lax.optimization_barrier(jnp.mean(centred * centred, -1, keepdims=True)) + EPS)
    normed = centred * inv_std
    conv_in = (normed * norm_gain).astype(jnp.bfloat16)
    conv_wide = jnp.pad(conv_in.astype(jnp.float32), ((half_taps, half_taps), (0, 0)))
    conv_seg = seg_padded[reach_rows - half_taps:reach_rows + length + half_taps]
    same_taps = [(conv_seg[tap_index:tap_index + length] == seg_row)[:, None] for tap_index in range(KERNEL)]
    pre_act = jnp.broadcast_to(conv_bias, (length, width))
    for tap_index in range(KERNEL):
        pre_act = pre_act + conv_kernel[tap_index] * jnp.where(same_taps[tap_index], conv_wide[tap_index:tap_index + length], 0.0)
    gate_sig = jax.nn.sigmoid(pre_act)
    conv_out = (pre_act * gate_sig).astype(jnp.bfloat16)
    grad_pre = (cot_row.astype(jnp.float32) * gate_sig * (1.0 + pre_act * (1.0 - gate_sig))).astype(jnp.bfloat16)
    grad_pre_f = grad_pre.astype(jnp.float32)
    bias_part = lax.optimization_barrier(jnp.sum(grad_pre_f, 0))
    kernel_rows = []
    for tap_index in range(KERNEL):
        kernel_rows.append(lax.optimization_barrier(jnp.sum(jnp.where(same_taps[tap_index], conv_wide[tap_index:tap_index + length] * grad_pre_f, 0.0), 0)))
    kernel_part = jnp.stack(kernel_rows, 0)
    grad_wide = jnp.pad(grad_pre_f, ((half_taps, half_taps), (0, 0)))
    grad_in = jnp.zeros((length, width), jnp.float32)
    for tap_index in range(KERNEL):
        mirror = 2 * half_taps - tap_index
        grad_in = grad_in + conv_kernel[tap_index] * jnp.where(same_taps[mirror], grad_wide[mirror:mirror + length], 0.0)
    gain_part = lax.optimization_barrier(jnp.sum(grad_in * normed, 0))
    grad_norm = grad_in * norm_gain
    grad_context = ((grad_norm - lax.optimization_barrier(jnp.mean(grad_norm, -1, keepdims=True)) - normed * lax.optimization_barrier(jnp.mean(grad_norm * normed, -1, keepdims=True))) * inv_std).astype(jnp.bfloat16)
    row_delta = lax.optimization_barrier(jnp.sum((grad_context.astype(jnp.float32) * context_f).reshape(length, HEADS, HEAD_DIM), -1)).T
    grad_heads = grad_context.reshape(length, HEADS, HEAD_DIM)

    def query_one(start_row):
        own_seg = lax.dynamic_slice_in_dim(seg_row, start_row, frame_count)
        wide_seg = lax.dynamic_slice_in_dim(seg_padded, start_row, wide_count)
        key_rows = lax.dynamic_slice_in_dim(key_padded, start_row, wide_count)
        prob_low, grad_logit = back_terms(lax.dynamic_slice_in_dim(query_heads, start_row, frame_count), key_rows, lax.dynamic_slice_in_dim(value_padded, start_row, wide_count), lax.dynamic_slice_in_dim(grad_heads, start_row, frame_count), lax.dynamic_slice_in_dim(total_rows, start_row, frame_count, 1), lax.dynamic_slice_in_dim(row_delta, start_row, frame_count, 1), own_seg[:, None] == wide_seg[None, :])
        return jnp.einsum('hqk,khe->qhe', grad_logit.astype(jnp.float32), key_rows.astype(jnp.float32))
    query_grad = lax.map(query_one, starts).reshape(length, width).astype(jnp.bfloat16)
    query_padded = pad_rows(query_heads)
    grad_padded = pad_rows(grad_heads)
    total_padded = jnp.pad(total_rows, ((0, 0), (reach_rows, reach_rows)))
    delta_padded = jnp.pad(row_delta, ((0, 0), (reach_rows, reach_rows)))

    def key_one(start_row):
        own_seg = lax.dynamic_slice_in_dim(seg_row, start_row, frame_count)
        wide_seg = lax.dynamic_slice_in_dim(seg_padded, start_row, wide_count)
        query_rows = lax.dynamic_slice_in_dim(query_padded, start_row, wide_count)
        grad_rows = lax.dynamic_slice_in_dim(grad_padded, start_row, wide_count)
        prob_low, grad_logit = back_terms(query_rows, lax.dynamic_slice_in_dim(key_heads, start_row, frame_count), lax.dynamic_slice_in_dim(value_heads, start_row, frame_count), grad_rows, lax.dynamic_slice_in_dim(total_padded, start_row, wide_count, 1), lax.dynamic_slice_in_dim(delta_padded, start_row, wide_count, 1), wide_seg[:, None] == own_seg[None, :])
        key_part = jnp.einsum('hqk,qhe->khe', grad_logit.astype(jnp.float32), query_rows.astype(jnp.float32))
        value_part = jnp.einsum('hqk,qhe->khe', prob_low.astype(jnp.float32), grad_rows.astype(jnp.float32))
        return (key_part, value_part)
    key_blocks, value_blocks = lax.map(key_one, starts)
    key_grad = key_blocks.reshape(length, width).astype(jnp.bfloat16)
    value_grad = value_blocks.reshape(length, width).astype(jnp.bfloat16)
    return (conv_out, query_grad, key_grad, value_grad, gain_part, kernel_part, bias_part)

def reference(queries, keys, values, segment_ids, norm_gain, conv_kernel, conv_bias, cotangent):

    def one_row(operands):
        return row_pass(operands, norm_gain, conv_kernel, conv_bias)
    results = lax.map(one_row, (queries, keys, values, segment_ids, cotangent))
    conv_out, query_grad, key_grad, value_grad, gain_rows, kernel_rows, bias_rows = results
    norm_factor = (BATCH * SEQLEN) ** (-0.5)
    return (conv_out, query_grad, key_grad, value_grad, lax.optimization_barrier(jnp.sum(gain_rows, 0)) * norm_factor, lax.optimization_barrier(jnp.sum(kernel_rows, 0)) * norm_factor, lax.optimization_barrier(jnp.sum(bias_rows, 0)) * norm_factor)
```

```python
import functools

import jax
import jax.numpy as jnp
from jax import lax
from jax.experimental import pallas as pl
from jax.experimental.pallas import tpu as pltpu
from jax.sharding import PartitionSpec as P

BF = jnp.bfloat16
F32 = jnp.float32
HEADS = 24
HEAD_DIM = 64
TAPS = 31
FR = 128
WIDE = 384
LANES = 128
PAIRS = HEADS * HEAD_DIM // LANES
WIDTH = HEADS * HEAD_DIM
EPS = 1e-05
NEG = -1e30
LOG2E = 1.4426950408889634
SCALE = HEAD_DIM ** (-0.5)
NX = 4
NC = 2
TILES = PAIRS * 4
HALF_TILES = TILES // NC
PIECE = HALF_TILES // NX
MESH = pl.DeviceIdType.MESH


def lanes_of(p):
    return pl.ds(pl.multiple_of(p * LANES, LANES), LANES)


def dot_nt(a, b):
    return lax.dot_general(a, b, (((1,), (1,)), ((), ())), preferred_element_type=F32)


def dot_nn(a, b):
    return lax.dot_general(a, b, (((1,), (0,)), ((), ())), preferred_element_type=F32)


def kernel(
    nz,
    ny,
    q_hbm,
    k_hbm,
    v_hbm,
    cot_hbm,
    seg_hbm,
    gain_ref,
    ker_ref,
    bias_ref,
    conv_hbm,
    dq_hbm,
    dk_hbm,
    dv_hbm,
    gain_out,
    ker_out,
    bias_out,
    kbuf,
    vbuf,
    qbuf,
    cotbuf,
    segbuf,
    segc,
    maskb,
    cm,
    wb,
    bb,
    gb,
    pbuf,
    ctx,
    ctxt,
    xbuf,
    gbuf,
    meanb,
    invb,
    acc1,
    acc2,
    xsend,
    xrecv,
    gsend,
    grecv,
    kg,
    dkv_own,
    dkv_send,
    dkv_recv,
    dq_buf,
    conv_buf,
    red,
    core_in,
    half,
    xg,
    other_in,
    tot,
    x_in,
    z_in,
    y_in,
    lsem,
    osem,
    kv_s,
    kv_r,
    xs,
    xr,
    gs,
    gr,
    d_s,
    d_r,
    c_s,
    c_r,
    x_s,
    x_r,
    z_s,
    z_r,
    y_s,
    y_r,
    ax_s,
    ax_r,
    ac_s,
    ac_r,
):
    nseq = nz * NX * NC
    me = lax.axis_index("seq")
    row = lax.axis_index("dp")
    right = lax.rem(me + 1, nseq)
    left = lax.rem(me + nseq - 1, nseq)
    core = lax.rem(me, NC)
    mx = lax.rem(me // NC, NX)
    mz = me // (NC * NX)

    def seq_dev(s):
        return (row, s)

    def x_dev(k):
        return seq_dev(mz * (NC * NX) + lax.rem(mx + k, NX) * NC + core)

    def z_dev(k):
        return seq_dev(lax.rem(mz + k, nz) * (NC * NX) + lax.rem(me, NC * NX))

    def y_dev(k):
        return (lax.rem(row + k, ny), me)

    core_dev = seq_dev(me + 1 - 2 * core)
    sides = (seq_dev(right), seq_dev(left))

    def remote(src, dst, s, r, dev):
        return pltpu.make_async_remote_copy(
            src_ref=src, dst_ref=dst, send_sem=s, recv_sem=r, device_id=dev, device_id_type=MESH
        )

    own = pl.ds(FR, FR)
    locals_ = [
        pltpu.make_async_copy(k_hbm, kbuf.at[own, :], lsem.at[0]),
        pltpu.make_async_copy(v_hbm, vbuf.at[own, :], lsem.at[1]),
        pltpu.make_async_copy(q_hbm, qbuf, lsem.at[2]),
        pltpu.make_async_copy(cot_hbm, cotbuf, lsem.at[3]),
    ]
    for j, blk in enumerate((left, me, right)):
        locals_.append(
            pltpu.make_async_copy(
                seg_hbm.at[:, pl.ds(pl.multiple_of(blk * FR, FR), FR)],
                segbuf.at[j],
                lsem.at[4 + j],
            )
        )
    for copy in locals_[::-1]:
        copy.start()

    barrier = pltpu.get_barrier_semaphore()
    partners = list(sides)
    partners += [x_dev(k) for k in range(1, NX)]
    partners += [z_dev(k) for k in range(1, nz)]
    partners += [y_dev(k) for k in range(1, ny)]
    for dev in partners:
        pl.semaphore_signal(barrier, inc=1, device_id=dev, device_id_type=MESH)
    pl.semaphore_wait(barrier, len(partners))

    def kv_copy(side, kv, p):
        src = (k_hbm, v_hbm)[kv]
        dst = (kbuf, vbuf)[kv]
        at = 0 if side == 0 else 2 * FR
        return remote(
            src.at[:, lanes_of(p)],
            dst.at[pl.ds(at, FR), lanes_of(p)],
            kv_s.at[side, kv, p],
            kv_r.at[side, kv, p],
            sides[side],
        )

    @pl.loop(0, PAIRS)
    def _(p):
        for kv in range(2):
            for side in range(2):
                kv_copy(side, kv, p).start()

    for j in range(3):
        locals_[4 + j].wait()
    own_row = segbuf[1]
    for j in range(3):
        col = jnp.broadcast_to(segbuf[j], (FR, LANES)).T
        segc[pl.ds(j * FR, FR), :] = col
        maskb[pl.ds(j * FR, FR), :] = jnp.where(col == own_row, 0.0, NEG)
    own_col = segc[pl.ds(FR, FR), :]
    for t in range(TAPS):
        cm[t] = jnp.where(segc[pl.ds(FR + t - 15, FR), :] == own_col, 1.0, 0.0)

    @pl.loop(0, PAIRS)
    def _(c):
        for t in range(TAPS):
            wb[c, t] = jnp.broadcast_to(ker_ref[t : t + 1, lanes_of(c)], (8, LANES))
        bb[c] = jnp.broadcast_to(bias_ref[:, lanes_of(c)], (8, LANES))
        gb[c] = jnp.broadcast_to(gain_ref[:, lanes_of(c)], (8, LANES))
        kg[c] = jnp.zeros_like(kg[c])

    for j in range(3):
        locals_[j].wait()
    low = lax.broadcasted_iota(jnp.int32, (FR, LANES), 1) < HEAD_DIM

    def diag(block):
        zero = jnp.zeros_like(block)
        return jnp.concatenate([jnp.where(low, block, zero), jnp.where(low, zero, block)], 0)

    def pick(block):
        return jnp.concatenate([block[:HEAD_DIM, :LANES], block[HEAD_DIM:, LANES:]], 0)

    @pl.loop(0, PAIRS)
    def _(p):
        for kv in range(2):
            for side in range(2):
                kv_copy(side, kv, p).wait_recv()
        key = kbuf[:, lanes_of(p)]
        val = vbuf[:, lanes_of(p)]
        qd = diag(qbuf[:, lanes_of(p)])
        mask = maskb[...]
        s = dot_nt(key, qd) * (SCALE * LOG2E) + jnp.concatenate([mask, mask], 1)
        top = jnp.max(s, 0, keepdims=True)
        e = jnp.exp2(s - top)
        inv = 1.0 / jnp.sum(e, 0, keepdims=True)
        prob = (e * inv).astype(BF)
        pbuf[p] = prob
        ct = pick(dot_nn(val.T, prob)).astype(BF).astype(F32)
        ctxt[p] = ct
        ctx[p] = ct.T

    zero = jnp.zeros((FR, LANES), F32)
    total = lax.fori_loop(0, PAIRS, lambda c, a: a + ctx[c], zero)
    mean = jnp.broadcast_to(jnp.sum(total, 1, keepdims=True) * (1.0 / WIDTH), (FR, LANES))
    meanb[...] = mean

    def square(c, a):
        d = ctx[c] - meanb[...]
        return a + d * d

    total = lax.fori_loop(0, PAIRS, square, zero)
    var = jnp.sum(total, 1, keepdims=True) * (1.0 / WIDTH)
    invb[...] = jnp.broadcast_to(lax.rsqrt(var + EPS), (FR, LANES))

    @pl.loop(0, PAIRS)
    def _(c):
        normed = (ctx[c] - meanb[...]) * invb[...]
        ctx[c] = normed
        x = (normed.reshape(16, 8, LANES) * gb[c][None]).reshape(FR, LANES).astype(BF)
        xsend[1, c] = x[:16]
        xsend[0, c] = x[FR - 16 :]
        xbuf[c, pl.ds(16, FR), :] = x.astype(F32)

    def x_copy(side):
        return remote(xsend.at[side], xrecv.at[side], xs.at[side], xr.at[side], sides[side])

    def g_copy(side):
        return remote(gsend.at[side], grecv.at[side], gs.at[side], gr.at[side], sides[side])

    for side in range(2):
        x_copy(side).start()
    locals_[3].wait()

    def conv_group(chunks, tiles):
        acc = [[bb[c] for _ in tiles] for c in chunks]
        for t in range(TAPS):
            ms = [cm[t, pl.ds(r, 8), :] for r in tiles]
            for j, c in enumerate(chunks):
                w = wb[c, t]
                for i, r in enumerate(tiles):
                    acc[j][i] = acc[j][i] + w * (ms[i] * xbuf[c, pl.ds(r + t + 1, 8), :])
        gr_ = []
        for j, c in enumerate(chunks):
            gr_.append([])
            for i, r in enumerate(tiles):
                a = acc[j][i]
                sig = 1.0 / (1.0 + jnp.exp(-a))
                acc[j][i] = a * sig
                gr_[j].append(sig * (1.0 + a * (1.0 - sig)))
        bias_sum = []
        for j, c in enumerate(chunks):
            for h in range(0, len(tiles), 2):
                r = tiles[h]
                out = jnp.concatenate(acc[j][h : h + 2], 0).astype(BF)
                conv_buf[pl.ds(r, 16), lanes_of(c)] = out
                g = jnp.concatenate(gr_[j][h : h + 2], 0)
                g = (g * cotbuf[pl.ds(r, 16), lanes_of(c)].astype(F32)).astype(BF)
                if isinstance(r, int) and r == 0:
                    gsend[1, c] = g
                elif isinstance(r, int) and r == FR - 16:
                    gsend[0, c] = g
                g = g.astype(F32)
                gbuf[c, pl.ds(r + 16, 16), :] = g
                gr_[j][h] = g[:8]
                gr_[j][h + 1] = g[8:]
            kg[c, TAPS] = kg[c, TAPS] + functools.reduce(jnp.add, gr_[j])
        for t in range(TAPS):
            ms = [cm[t, pl.ds(r, 8), :] for r in tiles]
            for j, c in enumerate(chunks):
                terms = [
                    gr_[j][i] * (ms[i] * xbuf[c, pl.ds(r + t + 1, 8), :])
                    for i, r in enumerate(tiles)
                ]
                kg[c, t] = kg[c, t] + functools.reduce(jnp.add, terms)

    edges = [0, 8, FR - 16, FR - 8]

    @pl.loop(0, PAIRS // 2)
    def _(cc):
        @pl.loop(0, 3)
        def _(rr):
            r0 = pl.multiple_of(rr * 32 + 16, 16)
            conv_group([2 * cc, 2 * cc + 1], [pl.multiple_of(r0 + 8 * i, 8) for i in range(4)])

    for side in range(2):
        x_copy(side).wait_recv()

    @pl.loop(0, PAIRS // 2)
    def _(cc):
        for c in (2 * cc, 2 * cc + 1):
            xbuf[c, pl.ds(0, 16), :] = xrecv[0, c].astype(F32)
            xbuf[c, pl.ds(FR + 16, 16), :] = xrecv[1, c].astype(F32)
        conv_group([2 * cc, 2 * cc + 1], edges)

    for side in range(2):
        g_copy(side).start()

    @pl.loop(0, PAIRS)
    def _(c):
        for rg in range(4):
            red[rg * PAIRS + c] = jnp.sum(kg[c, pl.ds(rg * 8, 8)], 1)

    conv_done = pltpu.make_async_copy(conv_buf, conv_hbm, osem.at[0])
    conv_done.start()

    other = (1 - core) * HALF_TILES
    mine = core * HALF_TILES
    core_copy = remote(red.at[pl.ds(other, HALF_TILES)], core_in, c_s, c_r, core_dev)
    core_copy.start()

    def in_group(chunks, tiles):
        acc = [[None for _ in tiles] for c in chunks]
        for u in range(TAPS):
            ms = [cm[u, pl.ds(r, 8), :] for r in tiles]
            for j, c in enumerate(chunks):
                w = wb[c, TAPS - 1 - u]
                for i, r in enumerate(tiles):
                    term = w * (ms[i] * gbuf[c, pl.ds(r + u + 1, 8), :])
                    acc[j][i] = term if u == 0 else acc[j][i] + term
        for i, r in enumerate(tiles):
            s1 = acc1[pl.ds(r, 8), :]
            s2 = acc2[pl.ds(r, 8), :]
            for j, c in enumerate(chunks):
                g = acc[j][i] * gb[c]
                dkv_own[0, c, pl.ds(r, 8), :] = g
                s1 = s1 + g
                s2 = s2 + g * ctx[c, pl.ds(r, 8), :]
            acc1[pl.ds(r, 8), :] = s1
            acc2[pl.ds(r, 8), :] = s2

    acc1[...] = zero
    acc2[...] = zero

    @pl.loop(0, PAIRS // 2)
    def _(cc):
        @pl.loop(0, 3)
        def _(rr):
            r0 = pl.multiple_of(rr * 32 + 16, 16)
            in_group([2 * cc, 2 * cc + 1], [pl.multiple_of(r0 + 8 * i, 8) for i in range(4)])

    core_copy.wait_recv()

    @pl.loop(0, HALF_TILES)
    def _(i):
        half[i] = red[mine + i] + core_in[i]

    def x_red(k):
        to = lax.rem(mx + k, NX)
        return remote(
            half.at[pl.ds(to * PIECE, PIECE)], x_in.at[mx], x_s.at[k - 1], x_r.at[k - 1], x_dev(k)
        )

    for k in range(1, NX):
        x_red(k).start()
    x_in[mx] = half[pl.ds(mx * PIECE, PIECE)]

    for side in range(2):
        g_copy(side).wait_recv()

    @pl.loop(0, PAIRS // 2)
    def _(cc):
        for c in (2 * cc, 2 * cc + 1):
            gbuf[c, pl.ds(0, 16), :] = grecv[0, c].astype(F32)
            gbuf[c, pl.ds(FR + 16, 16), :] = grecv[1, c].astype(F32)
        in_group([2 * cc, 2 * cc + 1], edges)

    acc1[...] = jnp.broadcast_to(jnp.sum(acc1[...], 1, keepdims=True) * (1.0 / WIDTH), (FR, LANES))
    acc2[...] = jnp.broadcast_to(jnp.sum(acc2[...], 1, keepdims=True) * (1.0 / WIDTH), (FR, LANES))

    def d_copy(side, kv, p):
        return remote(
            dkv_send.at[side, kv, :, lanes_of(p)],
            dkv_recv.at[side, kv, :, lanes_of(p)],
            d_s.at[side, kv, p],
            d_r.at[side, kv, p],
            sides[side],
        )

    def back(p):
        dc = (dkv_own[0, p] - acc1[...] - ctx[p] * acc2[...]) * invb[...]
        dc = dc.astype(BF)
        prod = dc.astype(F32).T * ctxt[p]
        delta = jnp.concatenate(
            [
                jnp.sum(prod[:HEAD_DIM], 0, keepdims=True),
                jnp.sum(prod[HEAD_DIM:], 0, keepdims=True),
            ],
            1,
        )
        key = kbuf[:, lanes_of(p)]
        val = vbuf[:, lanes_of(p)]
        dcd = diag(dc)
        qd = diag(qbuf[:, lanes_of(p)])
        prob = pbuf[p]
        dp = dot_nt(val, dcd)
        ds = (prob.astype(F32) * ((dp - delta) * SCALE)).astype(BF)
        dv = dot_nn(prob, dcd)
        dk = dot_nn(ds, qd)
        dq = pick(dot_nn(key.T, ds)).T
        dq_buf[:, lanes_of(p)] = dq.astype(BF)
        for kv, d in enumerate((dk, dv)):
            dkv_send[1, kv, :, lanes_of(p)] = d[:FR].astype(BF)
            dkv_own[kv, p] = d[FR : 2 * FR]
            dkv_send[0, kv, :, lanes_of(p)] = d[2 * FR :].astype(BF)
        for kv in range(2):
            for side in range(2):
                d_copy(side, kv, p).start()

    pl.loop(0, 3)(back)

    for k in range(1, NX):
        x_red(k).wait_recv()
    z_in[mz] = (x_in[0] + x_in[1]) + (x_in[2] + x_in[3])

    def z_copy(k):
        return remote(z_in.at[mz], z_in.at[mz], z_s.at[k - 1], z_r.at[k - 1], z_dev(k))

    def y_copy(k):
        return remote(y_in.at[row], y_in.at[row], y_s.at[k - 1], y_r.at[k - 1], y_dev(k))

    far_z = sorted(range(1, nz), key=lambda k: -min(k, nz - k))
    far_y = sorted(range(1, ny), key=lambda k: -min(k, ny - k))
    for k in far_z:
        z_copy(k).start()

    pl.loop(3, 8)(back)

    for k in far_z:
        z_copy(k).wait_recv()
    y_in[row] = functools.reduce(jnp.add, [z_in[i] for i in range(nz)])
    for k in far_y:
        y_copy(k).start()

    pl.loop(8, PAIRS)(back)

    dq_done = pltpu.make_async_copy(dq_buf, dq_hbm, osem.at[1])
    dq_done.start()

    for k in far_y:
        y_copy(k).wait_recv()
    xg[pl.ds(mx * PIECE, PIECE)] = functools.reduce(jnp.add, [y_in[i] for i in range(ny)])

    def x_gather(k):
        here = pl.ds(mx * PIECE, PIECE)
        return remote(xg.at[here], xg.at[here], ax_s.at[k - 1], ax_r.at[k - 1], x_dev(k))

    for k in range(1, NX):
        x_gather(k).start()

    @pl.loop(0, PAIRS)
    def _(p):
        for kv in range(2):
            for side in range(2):
                d_copy(side, kv, p).wait_recv()
            d = dkv_own[kv, p]
            d = d + dkv_recv[0, kv, :, lanes_of(p)].astype(F32)
            d = d + dkv_recv[1, kv, :, lanes_of(p)].astype(F32)
            (kbuf, vbuf)[kv][pl.ds(FR, FR), lanes_of(p)] = d.astype(BF)

    dk_done = pltpu.make_async_copy(kbuf.at[own, :], dk_hbm, osem.at[2])
    dv_done = pltpu.make_async_copy(vbuf.at[own, :], dv_hbm, osem.at[3])
    dk_done.start()
    dv_done.start()

    for k in range(1, NX):
        x_gather(k).wait_recv()
    gather_copy = remote(xg, other_in, ac_s, ac_r, core_dev)
    gather_copy.start()
    gather_copy.wait_recv()
    factor = (ny * nseq * FR) ** (-0.5)

    @pl.loop(0, HALF_TILES)
    def _(i):
        tot[mine + i] = xg[i]
        tot[other + i] = other_in[i]

    for c in range(PAIRS):
        at = slice(c * LANES, (c + 1) * LANES)
        gsum = jnp.zeros((8, LANES), F32)
        for rg in range(4):
            tile = tot[rg * PAIRS + c] * factor
            if rg < 3:
                ker_out[rg * 8 : rg * 8 + 8, at] = tile
                gsum = gsum + tile * ker_ref[rg * 8 : rg * 8 + 8, at]
            else:
                ker_out[24:31, at] = tile[:7]
                bias_out[:, at] = tile[7:]
                gsum = gsum + jnp.concatenate(
                    [tile[:7] * ker_ref[24:31, at], jnp.zeros((1, LANES), F32)], 0
                )
        gain_out[:, at] = jnp.sum(gsum, 0, keepdims=True) / gain_ref[:, at]

    @pl.loop(0, PAIRS)
    def _(p):
        for kv in range(2):
            for side in range(2):
                kv_copy(side, kv, p).wait_send()
                d_copy(side, kv, p).wait_send()

    for side in range(2):
        x_copy(side).wait_send()
        g_copy(side).wait_send()
    for k in range(1, NX):
        x_red(k).wait_send()
        x_gather(k).wait_send()
    for k in far_z:
        z_copy(k).wait_send()
    for k in far_y:
        y_copy(k).wait_send()
    core_copy.wait_send()
    gather_copy.wait_send()
    conv_done.wait()
    dq_done.wait()
    dk_done.wait()
    dv_done.wait()


def per_device(nz, ny, queries, keys, values, segment_ids, norm_gain, conv_kernel, conv_bias, cot):
    dma = pltpu.SemaphoreType.DMA
    vmem = pltpu.VMEM
    any_ = pl.BlockSpec(memory_space=pl.ANY)
    whole = pl.BlockSpec(memory_space=pltpu.VMEM)
    row = jax.ShapeDtypeStruct((FR, WIDTH), BF)
    outs = pl.pallas_call(
        functools.partial(kernel, nz, ny),
        out_shape=(
            row,
            row,
            row,
            row,
            jax.ShapeDtypeStruct((1, WIDTH), F32),
            jax.ShapeDtypeStruct((TAPS, WIDTH), F32),
            jax.ShapeDtypeStruct((1, WIDTH), F32),
        ),
        in_specs=[any_] * 5 + [whole] * 3,
        out_specs=(any_, any_, any_, any_, whole, whole, whole),
        scratch_shapes=[
            vmem((WIDE, WIDTH), BF),
            vmem((WIDE, WIDTH), BF),
            vmem((FR, WIDTH), BF),
            vmem((FR, WIDTH), BF),
            vmem((3, 1, FR), jnp.int32),
            vmem((WIDE, LANES), jnp.int32),
            vmem((WIDE, LANES), F32),
            vmem((TAPS, FR, LANES), F32),
            vmem((PAIRS, TAPS, 8, LANES), F32),
            vmem((PAIRS, 8, LANES), F32),
            vmem((PAIRS, 8, LANES), F32),
            vmem((PAIRS, WIDE, 2 * LANES), BF),
            vmem((PAIRS, FR, LANES), F32),
            vmem((PAIRS, FR, LANES), F32),
            vmem((PAIRS, FR + 32, LANES), F32),
            vmem((PAIRS, FR + 32, LANES), F32),
            vmem((FR, LANES), F32),
            vmem((FR, LANES), F32),
            vmem((FR, LANES), F32),
            vmem((FR, LANES), F32),
            vmem((2, PAIRS, 16, LANES), BF),
            vmem((2, PAIRS, 16, LANES), BF),
            vmem((2, PAIRS, 16, LANES), BF),
            vmem((2, PAIRS, 16, LANES), BF),
            vmem((PAIRS, 32, 8, LANES), F32),
            vmem((2, PAIRS, FR, LANES), F32),
            vmem((2, 2, FR, WIDTH), BF),
            vmem((2, 2, FR, WIDTH), BF),
            vmem((FR, WIDTH), BF),
            vmem((FR, WIDTH), BF),
            vmem((TILES, 8, LANES), F32),
            vmem((HALF_TILES, 8, LANES), F32),
            vmem((HALF_TILES, 8, LANES), F32),
            vmem((HALF_TILES, 8, LANES), F32),
            vmem((HALF_TILES, 8, LANES), F32),
            vmem((TILES, 8, LANES), F32),
            vmem((NX, PIECE, 8, LANES), F32),
            vmem((nz, PIECE, 8, LANES), F32),
            vmem((ny, PIECE, 8, LANES), F32),
            dma((7,)),
            dma((4,)),
            dma((2, 2, PAIRS)),
            dma((2, 2, PAIRS)),
            dma((2,)),
            dma((2,)),
            dma((2,)),
            dma((2,)),
            dma((2, 2, PAIRS)),
            dma((2, 2, PAIRS)),
            dma,
            dma,
            dma((NX - 1,)),
            dma((NX - 1,)),
            dma((nz - 1,)),
            dma((nz - 1,)),
            dma((ny - 1,)),
            dma((ny - 1,)),
            dma((NX - 1,)),
            dma((NX - 1,)),
            dma,
            dma,
        ],
        compiler_params=pltpu.CompilerParams(
            collective_id=0, has_side_effects=True, vmem_limit_bytes=56 * 1024 * 1024
        ),
    )(
        queries[0],
        keys[0],
        values[0],
        cot[0],
        segment_ids,
        norm_gain.reshape(1, WIDTH),
        conv_kernel,
        conv_bias.reshape(1, WIDTH),
    )
    conv_out, dq, dk, dv, gain, ker, bias = outs
    return (
        conv_out[None],
        dq[None],
        dk[None],
        dv[None],
        gain.reshape(WIDTH),
        ker,
        bias.reshape(WIDTH),
    )


def solution(mesh):
    rows = P("dp", "seq", None)
    nz = mesh.shape["seq"] // (NX * NC)
    return jax.shard_map(
        functools.partial(per_device, nz, mesh.shape["dp"]),
        mesh=mesh,
        in_specs=(rows, rows, rows, P("dp", None), P(), P(), P(), rows),
        out_specs=(rows, rows, rows, rows, P(), P(), P()),
        check_vma=False,
    )
```

```python
import functools

import jax
import jax.numpy as jnp
from jax import lax
from jax.experimental import pallas as pl
from jax.experimental.pallas import tpu as pltpu
from jax.sharding import PartitionSpec as P

BF = jnp.bfloat16
F32 = jnp.float32
HEADS = 24
HEAD_DIM = 64
TAPS = 31
FR = 128
WIDE = 384
LANES = 128
PAIRS = HEADS * HEAD_DIM // LANES
WIDTH = HEADS * HEAD_DIM
EPS = 1e-05
NEG = -1e30
LOG2E = 1.4426950408889634
SCALE = HEAD_DIM ** (-0.5)
NX = 4
NC = 2
GROUP = NX * NC
TILES = PAIRS * 4
PIECE = TILES // GROUP
PART = PIECE // 2
MESH = pl.DeviceIdType.MESH


def lanes_of(p):
    return pl.ds(pl.multiple_of(p * LANES, LANES), LANES)


def dot_nt(a, b):
    return lax.dot_general(a, b, (((1,), (1,)), ((), ())), preferred_element_type=F32)


def dot_nn(a, b):
    return lax.dot_general(a, b, (((1,), (0,)), ((), ())), preferred_element_type=F32)


def kernel(
    nz,
    ny,
    q_hbm,
    k_hbm,
    v_hbm,
    cot_hbm,
    seg_hbm,
    gain_hbm,
    ker_hbm,
    bias_hbm,
    conv_hbm,
    dq_hbm,
    dk_hbm,
    dv_hbm,
    sums_hbm,
    gain_ref,
    ker_ref,
    bias_ref,
    kbuf,
    vbuf,
    qbuf,
    cotbuf,
    segbuf,
    segc,
    maskb,
    cm,
    wb,
    bb,
    gb,
    pbuf,
    ctx,
    ctxt,
    xbuf,
    gbuf,
    meanb,
    invb,
    acc1,
    acc2,
    xsend,
    xrecv,
    gsend,
    grecv,
    kg,
    dkv_own,
    dkv_send,
    dkv_recv,
    dq_buf,
    conv_buf,
    red,
    r_in,
    za_in,
    yb_in,
    ya_in,
    zb_in,
    sums,
    lsem,
    osem,
    kv_s,
    kv_r,
    xs,
    xr,
    gs,
    gr,
    d_s,
    d_r,
    r_s,
    r_r,
    z_s,
    z_r,
    y_s,
    y_r,
    a_s,
    a_r,
):
    nseq = nz * NX * NC
    me = lax.axis_index("seq")
    row = lax.axis_index("dp")
    right = lax.rem(me + 1, nseq)
    left = lax.rem(me + nseq - 1, nseq)
    mg = lax.rem(me, GROUP)
    mz = me // GROUP

    def seq_dev(s):
        return (row, s)

    def g_dev(k):
        return seq_dev(mz * GROUP + lax.rem(mg + k, GROUP))

    def z_dev(k):
        return seq_dev(lax.rem(mz + k, nz) * GROUP + mg)

    def y_dev(k):
        return (lax.rem(row + k, ny), me)

    far_g = [4, 3, 5, 2, 6, 1, 7]
    far_z = sorted(range(1, nz), key=lambda k: -min(k, nz - k))
    far_y = sorted(range(1, ny), key=lambda k: -min(k, ny - k))
    sides = (seq_dev(right), seq_dev(left))

    def remote(src, dst, s, r, dev):
        return pltpu.make_async_remote_copy(
            src_ref=src, dst_ref=dst, send_sem=s, recv_sem=r, device_id=dev, device_id_type=MESH
        )

    own = pl.ds(FR, FR)
    locals_ = [
        pltpu.make_async_copy(k_hbm, kbuf.at[own, :], lsem.at[0]),
        pltpu.make_async_copy(v_hbm, vbuf.at[own, :], lsem.at[1]),
        pltpu.make_async_copy(q_hbm, qbuf, lsem.at[2]),
        pltpu.make_async_copy(cot_hbm, cotbuf, lsem.at[3]),
    ]
    for j, blk in enumerate((left, me, right)):
        locals_.append(
            pltpu.make_async_copy(
                seg_hbm.at[:, pl.ds(pl.multiple_of(blk * FR, FR), FR)],
                segbuf.at[j],
                lsem.at[4 + j],
            )
        )
    locals_.append(pltpu.make_async_copy(gain_hbm, gain_ref, lsem.at[7]))
    locals_.append(pltpu.make_async_copy(ker_hbm, ker_ref, lsem.at[8]))
    locals_.append(pltpu.make_async_copy(bias_hbm, bias_ref, lsem.at[9]))

    barrier = pltpu.get_barrier_semaphore()
    partners = list(sides)
    partners += [g_dev(k) for k in far_g]
    partners += [z_dev(k) for k in far_z]
    partners += [y_dev(k) for k in far_y]
    for dev in partners:
        pl.semaphore_signal(barrier, inc=1, device_id=dev, device_id_type=MESH)
    for copy in locals_[::-1]:
        copy.start()
    pl.semaphore_wait(barrier, len(partners))

    def kv_copy(side, kv, p):
        src = (k_hbm, v_hbm)[kv]
        dst = (kbuf, vbuf)[kv]
        at = 0 if side == 0 else 2 * FR
        return remote(
            src.at[:, lanes_of(p)],
            dst.at[pl.ds(at, FR), lanes_of(p)],
            kv_s.at[side, kv, p],
            kv_r.at[side, kv, p],
            sides[side],
        )

    @pl.loop(0, PAIRS)
    def _(p):
        for kv in range(2):
            for side in range(2):
                kv_copy(side, kv, p).start()

    for j in range(3):
        locals_[4 + j].wait()
    own_row = segbuf[1]
    for j in range(3):
        col = jnp.broadcast_to(segbuf[j], (FR, LANES)).T
        segc[pl.ds(j * FR, FR), :] = col
        maskb[pl.ds(j * FR, FR), :] = jnp.where(col == own_row, 0.0, NEG)
    own_col = segc[pl.ds(FR, FR), :]
    for t in range(TAPS):
        cm[t] = jnp.where(segc[pl.ds(FR + t - 15, FR), :] == own_col, 1.0, 0.0)

    for j in range(7, 10):
        locals_[j].wait()

    @pl.loop(0, PAIRS)
    def _(c):
        for t in range(TAPS):
            wb[c, t] = jnp.broadcast_to(ker_ref[t : t + 1, lanes_of(c)], (8, LANES))
        bb[c] = jnp.broadcast_to(bias_ref[lanes_of(c)].reshape(1, LANES), (8, LANES))
        gb[c] = jnp.broadcast_to(gain_ref[lanes_of(c)].reshape(1, LANES), (8, LANES))
        kg[c] = jnp.zeros_like(kg[c])

    for j in range(3):
        locals_[j].wait()
    low = lax.broadcasted_iota(jnp.int32, (FR, LANES), 1) < HEAD_DIM

    def diag(block):
        zero = jnp.zeros_like(block)
        return jnp.concatenate([jnp.where(low, block, zero), jnp.where(low, zero, block)], 0)

    def pick(block):
        return jnp.concatenate([block[:HEAD_DIM, :LANES], block[HEAD_DIM:, LANES:]], 0)

    @pl.loop(0, PAIRS)
    def _(p):
        for kv in range(2):
            for side in range(2):
                kv_copy(side, kv, p).wait_recv()
        key = kbuf[:, lanes_of(p)]
        val = vbuf[:, lanes_of(p)]
        qd = diag(qbuf[:, lanes_of(p)])
        mask = maskb[...]
        s = dot_nt(key, qd) * (SCALE * LOG2E) + jnp.concatenate([mask, mask], 1)
        top = jnp.max(s, 0, keepdims=True)
        e = jnp.exp2(s - top)
        inv = 1.0 / jnp.sum(e, 0, keepdims=True)
        prob = (e * inv).astype(BF)
        pbuf[p] = prob
        ct = pick(dot_nn(val.T, prob)).astype(BF).astype(F32)
        ctxt[p] = ct
        ctx[p] = ct.T

    zero = jnp.zeros((FR, LANES), F32)
    total = lax.fori_loop(0, PAIRS, lambda c, a: a + ctx[c], zero)
    mean = jnp.broadcast_to(jnp.sum(total, 1, keepdims=True) * (1.0 / WIDTH), (FR, LANES))
    meanb[...] = mean

    def square(c, a):
        d = ctx[c] - meanb[...]
        return a + d * d

    total = lax.fori_loop(0, PAIRS, square, zero)
    var = jnp.sum(total, 1, keepdims=True) * (1.0 / WIDTH)
    invb[...] = jnp.broadcast_to(lax.rsqrt(var + EPS), (FR, LANES))

    @pl.loop(0, PAIRS)
    def _(c):
        normed = (ctx[c] - meanb[...]) * invb[...]
        ctx[c] = normed
        x = (normed.reshape(16, 8, LANES) * gb[c][None]).reshape(FR, LANES).astype(BF)
        xsend[1, c] = x[:16]
        xsend[0, c] = x[FR - 16 :]
        xbuf[c, pl.ds(16, FR), :] = x.astype(F32)

    def x_copy(side):
        return remote(xsend.at[side], xrecv.at[side], xs.at[side], xr.at[side], sides[side])

    def g_copy(side):
        return remote(gsend.at[side], grecv.at[side], gs.at[side], gr.at[side], sides[side])

    for side in range(2):
        x_copy(side).start()
    locals_[3].wait()

    def conv_group(chunks, tiles):
        acc = [[bb[c] for _ in tiles] for c in chunks]
        for t in range(TAPS):
            ms = [cm[t, pl.ds(r, 8), :] for r in tiles]
            for j, c in enumerate(chunks):
                w = wb[c, t]
                for i, r in enumerate(tiles):
                    acc[j][i] = acc[j][i] + w * (ms[i] * xbuf[c, pl.ds(r + t + 1, 8), :])
        gr_ = []
        for j, c in enumerate(chunks):
            gr_.append([])
            for i, r in enumerate(tiles):
                a = acc[j][i]
                sig = 1.0 / (1.0 + jnp.exp(-a))
                acc[j][i] = a * sig
                gr_[j].append(sig * (1.0 + a * (1.0 - sig)))
        bias_sum = []
        for j, c in enumerate(chunks):
            for h in range(0, len(tiles), 2):
                r = tiles[h]
                out = jnp.concatenate(acc[j][h : h + 2], 0).astype(BF)
                conv_buf[pl.ds(r, 16), lanes_of(c)] = out
                g = jnp.concatenate(gr_[j][h : h + 2], 0)
                g = (g * cotbuf[pl.ds(r, 16), lanes_of(c)].astype(F32)).astype(BF)
                if isinstance(r, int) and r == 0:
                    gsend[1, c] = g
                elif isinstance(r, int) and r == FR - 16:
                    gsend[0, c] = g
                g = g.astype(F32)
                gbuf[c, pl.ds(r + 16, 16), :] = g
                gr_[j][h] = g[:8]
                gr_[j][h + 1] = g[8:]
            kg[c, TAPS] = kg[c, TAPS] + functools.reduce(jnp.add, gr_[j])
        for t in range(TAPS):
            ms = [cm[t, pl.ds(r, 8), :] for r in tiles]
            for j, c in enumerate(chunks):
                terms = [
                    gr_[j][i] * (ms[i] * xbuf[c, pl.ds(r + t + 1, 8), :])
                    for i, r in enumerate(tiles)
                ]
                kg[c, t] = kg[c, t] + functools.reduce(jnp.add, terms)

    edges = [0, 8, FR - 16, FR - 8]

    @pl.loop(0, PAIRS // 2)
    def _(cc):
        @pl.loop(0, 3)
        def _(rr):
            r0 = pl.multiple_of(rr * 32 + 16, 16)
            conv_group([2 * cc, 2 * cc + 1], [pl.multiple_of(r0 + 8 * i, 8) for i in range(4)])

    for side in range(2):
        x_copy(side).wait_recv()

    @pl.loop(0, PAIRS // 2)
    def _(cc):
        for c in (2 * cc, 2 * cc + 1):
            xbuf[c, pl.ds(0, 16), :] = xrecv[0, c].astype(F32)
            xbuf[c, pl.ds(FR + 16, 16), :] = xrecv[1, c].astype(F32)
        conv_group([2 * cc, 2 * cc + 1], edges)

    for side in range(2):
        g_copy(side).start()

    @pl.loop(0, PAIRS)
    def _(c):
        for rg in range(4):
            red[rg * PAIRS + c] = jnp.sum(kg[c, pl.ds(rg * 8, 8)], 1).astype(BF)

    mine = pl.ds(mg * PIECE, PIECE)

    def r_copy(k):
        to = lax.rem(mg + k, GROUP)
        return remote(
            red.at[pl.ds(to * PIECE, PIECE)], r_in.at[mg], r_s.at[k - 1], r_r.at[k - 1], g_dev(k)
        )

    def z_copy(buf, j, k):
        return remote(buf.at[mz], buf.at[mz], z_s.at[j, k - 1], z_r.at[j, k - 1], z_dev(k))

    def y_copy(buf, j, k):
        return remote(buf.at[row], buf.at[row], y_s.at[j, k - 1], y_r.at[j, k - 1], y_dev(k))

    def a_copy(k):
        return remote(sums.at[mine], sums.at[mine], a_s.at[k - 1], a_r.at[k - 1], g_dev(k))

    def add_up(buf, count):
        return functools.reduce(jnp.add, [buf[i].astype(F32) for i in range(count)])

    for k in far_g:
        r_copy(k).start()
    r_in[mg] = red[mine]

    conv_done = pltpu.make_async_copy(conv_buf, conv_hbm, osem.at[0])
    conv_done.start()

    def in_group(chunks, tiles):
        acc = [[None for _ in tiles] for c in chunks]
        for u in range(TAPS):
            ms = [cm[u, pl.ds(r, 8), :] for r in tiles]
            for j, c in enumerate(chunks):
                w = wb[c, TAPS - 1 - u]
                for i, r in enumerate(tiles):
                    term = w * (ms[i] * gbuf[c, pl.ds(r + u + 1, 8), :])
                    acc[j][i] = term if u == 0 else acc[j][i] + term
        for i, r in enumerate(tiles):
            s1 = acc1[pl.ds(r, 8), :]
            s2 = acc2[pl.ds(r, 8), :]
            for j, c in enumerate(chunks):
                g = acc[j][i] * gb[c]
                dkv_own[0, c, pl.ds(r, 8), :] = g
                s1 = s1 + g
                s2 = s2 + g * ctx[c, pl.ds(r, 8), :]
            acc1[pl.ds(r, 8), :] = s1
            acc2[pl.ds(r, 8), :] = s2

    acc1[...] = zero
    acc2[...] = zero

    @pl.loop(0, PAIRS // 2)
    def _(cc):
        @pl.loop(0, 3)
        def _(rr):
            r0 = pl.multiple_of(rr * 32 + 16, 16)
            in_group([2 * cc, 2 * cc + 1], [pl.multiple_of(r0 + 8 * i, 8) for i in range(4)])

    for side in range(2):
        g_copy(side).wait_recv()

    @pl.loop(0, PAIRS // 2)
    def _(cc):
        for c in (2 * cc, 2 * cc + 1):
            gbuf[c, pl.ds(0, 16), :] = grecv[0, c].astype(F32)
            gbuf[c, pl.ds(FR + 16, 16), :] = grecv[1, c].astype(F32)
        in_group([2 * cc, 2 * cc + 1], edges)

    acc1[...] = jnp.broadcast_to(jnp.sum(acc1[...], 1, keepdims=True) * (1.0 / WIDTH), (FR, LANES))
    acc2[...] = jnp.broadcast_to(jnp.sum(acc2[...], 1, keepdims=True) * (1.0 / WIDTH), (FR, LANES))

    def d_copy(side, kv, p):
        return remote(
            dkv_send.at[side, kv, :, lanes_of(p)],
            dkv_recv.at[side, kv, :, lanes_of(p)],
            d_s.at[side, kv, p],
            d_r.at[side, kv, p],
            sides[side],
        )

    def back(p):
        dc = (dkv_own[0, p] - acc1[...] - ctx[p] * acc2[...]) * invb[...]
        dc = dc.astype(BF)
        prod = dc.astype(F32).T * ctxt[p]
        delta = jnp.concatenate(
            [
                jnp.sum(prod[:HEAD_DIM], 0, keepdims=True),
                jnp.sum(prod[HEAD_DIM:], 0, keepdims=True),
            ],
            1,
        )
        key = kbuf[:, lanes_of(p)]
        val = vbuf[:, lanes_of(p)]
        dcd = diag(dc)
        qd = diag(qbuf[:, lanes_of(p)])
        prob = pbuf[p]
        dp = dot_nt(val, dcd)
        ds = (prob.astype(F32) * ((dp - delta) * SCALE)).astype(BF)
        dv = dot_nn(prob, dcd)
        dk = dot_nn(ds, qd)
        dq = pick(dot_nn(key.T, ds)).T
        dq_buf[:, lanes_of(p)] = dq.astype(BF)
        for kv, d in enumerate((dk, dv)):
            dkv_send[1, kv, :, lanes_of(p)] = d[:FR].astype(BF)
            dkv_own[kv, p] = d[FR : 2 * FR]
            dkv_send[0, kv, :, lanes_of(p)] = d[2 * FR :].astype(BF)
        for kv in range(2):
            for side in range(2):
                d_copy(side, kv, p).start()

    for k in far_g:
        r_copy(k).wait_recv()
    part = add_up(r_in, GROUP).astype(BF)
    za_in[mz] = part[:PART]
    yb_in[row] = part[PART:]
    for k in far_z:
        z_copy(za_in, 0, k).start()
    for k in far_y:
        y_copy(yb_in, 0, k).start()

    pl.loop(0, 7)(back)

    for k in far_z:
        z_copy(za_in, 0, k).wait_recv()
    for k in far_y:
        y_copy(yb_in, 0, k).wait_recv()
    ya_in[row] = add_up(za_in, nz).astype(BF)
    zb_in[mz] = add_up(yb_in, ny).astype(BF)
    for k in far_y:
        y_copy(ya_in, 1, k).start()
    for k in far_z:
        z_copy(zb_in, 1, k).start()

    pl.loop(7, PAIRS)(back)

    dq_done = pltpu.make_async_copy(dq_buf, dq_hbm, osem.at[1])
    dq_done.start()

    for k in far_y:
        y_copy(ya_in, 1, k).wait_recv()
    for k in far_z:
        z_copy(zb_in, 1, k).wait_recv()
    sums[pl.ds(mg * PIECE, PART)] = add_up(ya_in, ny).astype(BF)
    sums[pl.ds(mg * PIECE + PART, PART)] = add_up(zb_in, nz).astype(BF)
    for k in far_g:
        a_copy(k).start()

    @pl.loop(0, PAIRS)
    def _(p):
        for kv in range(2):
            for side in range(2):
                d_copy(side, kv, p).wait_recv()
            d = dkv_own[kv, p]
            d = d + dkv_recv[0, kv, :, lanes_of(p)].astype(F32)
            d = d + dkv_recv[1, kv, :, lanes_of(p)].astype(F32)
            (kbuf, vbuf)[kv][pl.ds(FR, FR), lanes_of(p)] = d.astype(BF)

    dk_done = pltpu.make_async_copy(kbuf.at[own, :], dk_hbm, osem.at[2])
    dv_done = pltpu.make_async_copy(vbuf.at[own, :], dv_hbm, osem.at[3])
    dk_done.start()
    dv_done.start()

    for k in far_g:
        a_copy(k).wait_recv()
    sums_done = pltpu.make_async_copy(sums, sums_hbm, osem.at[4])
    sums_done.start()

    @pl.loop(0, PAIRS)
    def _(p):
        for kv in range(2):
            for side in range(2):
                kv_copy(side, kv, p).wait_send()
                d_copy(side, kv, p).wait_send()

    for side in range(2):
        x_copy(side).wait_send()
        g_copy(side).wait_send()
    for k in far_g:
        r_copy(k).wait_send()
        a_copy(k).wait_send()
    for k in far_z:
        z_copy(za_in, 0, k).wait_send()
        z_copy(zb_in, 1, k).wait_send()
    for k in far_y:
        y_copy(yb_in, 0, k).wait_send()
        y_copy(ya_in, 1, k).wait_send()
    sums_done.wait()
    conv_done.wait()
    dq_done.wait()
    dk_done.wait()
    dv_done.wait()


def finish(
    factor,
    conv_in,
    dq_in,
    dk_in,
    dv_in,
    sums_in,
    gain_hbm,
    ker_hbm,
    conv_out,
    dq_out,
    dk_out,
    dv_out,
    gain_out,
    ker_out,
    bias_out,
    gain_ref,
    ker_ref,
    sem,
):
    loads = [
        pltpu.make_async_copy(gain_hbm, gain_ref, sem.at[4]),
        pltpu.make_async_copy(ker_hbm, ker_ref, sem.at[5]),
    ]
    for copy in loads:
        copy.start()
    copies = [
        pltpu.make_async_copy(a, b, sem.at[i])
        for i, (a, b) in enumerate(
            ((conv_in, conv_out), (dq_in, dq_out), (dk_in, dk_out), (dv_in, dv_out))
        )
    ]
    for copy in copies:
        copy.start()
    for copy in loads:
        copy.wait()
    for c in range(PAIRS):
        at = slice(c * LANES, (c + 1) * LANES)
        gsum = jnp.zeros((8, LANES), F32)
        for rg in range(4):
            tile = sums_in[rg * PAIRS + c].astype(F32) * factor
            if rg < 3:
                ker_out[rg * 8 : rg * 8 + 8, at] = tile
                gsum = gsum + tile * ker_ref[rg * 8 : rg * 8 + 8, at]
            else:
                ker_out[24:31, at] = tile[:7]
                bias_out[at] = tile[7]
                gsum = gsum + jnp.concatenate(
                    [tile[:7] * ker_ref[24:31, at], jnp.zeros((1, LANES), F32)], 0
                )
        gain_out[at] = jnp.sum(gsum, 0) / gain_ref[at]
    for copy in copies:
        copy.wait()


def per_device(nz, ny, queries, keys, values, segment_ids, norm_gain, conv_kernel, conv_bias, cot):
    dma = pltpu.SemaphoreType.DMA
    vmem = pltpu.VMEM
    any_ = pl.BlockSpec(memory_space=pl.ANY)
    whole = pl.BlockSpec(memory_space=pltpu.VMEM)
    row = jax.ShapeDtypeStruct((FR, WIDTH), BF)
    in_hbm = functools.partial(pltpu.with_memory_space_constraint, memory_space=pltpu.HBM)
    rows = [in_hbm(a[0]) for a in (queries, keys, values, cot)]
    segment_ids, gain_in, ker_in, bias_in = map(
        in_hbm, (segment_ids, norm_gain, conv_kernel, conv_bias)
    )
    outs = pl.pallas_call(
        functools.partial(kernel, nz, ny),
        out_shape=(
            row,
            row,
            row,
            row,
            jax.ShapeDtypeStruct((TILES, 8, LANES), BF),
        ),
        in_specs=[any_] * 8,
        out_specs=(any_,) * 5,
        scratch_shapes=[
            vmem((WIDTH,), F32),
            vmem((TAPS, WIDTH), F32),
            vmem((WIDTH,), F32),
            vmem((WIDE, WIDTH), BF),
            vmem((WIDE, WIDTH), BF),
            vmem((FR, WIDTH), BF),
            vmem((FR, WIDTH), BF),
            vmem((3, 1, FR), jnp.int32),
            vmem((WIDE, LANES), jnp.int32),
            vmem((WIDE, LANES), F32),
            vmem((TAPS, FR, LANES), F32),
            vmem((PAIRS, TAPS, 8, LANES), F32),
            vmem((PAIRS, 8, LANES), F32),
            vmem((PAIRS, 8, LANES), F32),
            vmem((PAIRS, WIDE, 2 * LANES), BF),
            vmem((PAIRS, FR, LANES), F32),
            vmem((PAIRS, FR, LANES), F32),
            vmem((PAIRS, FR + 32, LANES), F32),
            vmem((PAIRS, FR + 32, LANES), F32),
            vmem((FR, LANES), F32),
            vmem((FR, LANES), F32),
            vmem((FR, LANES), F32),
            vmem((FR, LANES), F32),
            vmem((2, PAIRS, 16, LANES), BF),
            vmem((2, PAIRS, 16, LANES), BF),
            vmem((2, PAIRS, 16, LANES), BF),
            vmem((2, PAIRS, 16, LANES), BF),
            vmem((PAIRS, 32, 8, LANES), F32),
            vmem((2, PAIRS, FR, LANES), F32),
            vmem((2, 2, FR, WIDTH), BF),
            vmem((2, 2, FR, WIDTH), BF),
            vmem((FR, WIDTH), BF),
            vmem((FR, WIDTH), BF),
            vmem((TILES, 8, LANES), BF),
            vmem((GROUP, PIECE, 8, LANES), BF),
            vmem((nz, PART, 8, LANES), BF),
            vmem((ny, PART, 8, LANES), BF),
            vmem((ny, PART, 8, LANES), BF),
            vmem((nz, PART, 8, LANES), BF),
            vmem((TILES, 8, LANES), BF),
            dma((10,)),
            dma((5,)),
            dma((2, 2, PAIRS)),
            dma((2, 2, PAIRS)),
            dma((2,)),
            dma((2,)),
            dma((2,)),
            dma((2,)),
            dma((2, 2, PAIRS)),
            dma((2, 2, PAIRS)),
            dma((GROUP - 1,)),
            dma((GROUP - 1,)),
            dma((2, nz - 1)),
            dma((2, nz - 1)),
            dma((2, ny - 1)),
            dma((2, ny - 1)),
            dma((GROUP - 1,)),
            dma((GROUP - 1,)),
        ],
        compiler_params=pltpu.CompilerParams(
            collective_id=0, has_side_effects=True, vmem_limit_bytes=36 * 1024 * 1024
        ),
    )(
        *rows,
        segment_ids,
        gain_in,
        ker_in,
        bias_in,
    )
    factor = (ny * nz * GROUP * FR) ** (-0.5)
    vec = jax.ShapeDtypeStruct((WIDTH,), F32)
    conv_out, dq, dk, dv, gain, ker, bias = pl.pallas_call(
        functools.partial(finish, factor),
        out_shape=(row, row, row, row, vec, jax.ShapeDtypeStruct((TAPS, WIDTH), F32), vec),
        in_specs=[any_] * 4 + [whole] + [any_] * 2,
        out_specs=(any_,) * 4 + (whole,) * 3,
        scratch_shapes=[vmem((WIDTH,), F32), vmem((TAPS, WIDTH), F32), dma((6,))],
        compiler_params=pltpu.CompilerParams(vmem_limit_bytes=4 * 1024 * 1024),
    )(*outs, gain_in, ker_in)
    return (conv_out[None], dq[None], dk[None], dv[None], gain, ker, bias)


def solution(mesh):
    rows = P("dp", "seq", None)
    nz = mesh.shape["seq"] // (NX * NC)
    return jax.shard_map(
        functools.partial(per_device, nz, mesh.shape["dp"]),
        mesh=mesh,
        in_specs=(rows, rows, rows, P("dp", None), P(), P(), P(), rows),
        out_specs=(rows, rows, rows, rows, P(), P(), P()),
        check_vma=False,
    )
```

```python
import functools

import jax
import jax.numpy as jnp
from jax import lax
from jax.experimental import pallas as pl
from jax.experimental.pallas import tpu as pltpu
from jax.sharding import PartitionSpec as P

BF = jnp.bfloat16
F32 = jnp.float32
HEADS = 24
HEAD_DIM = 64
TAPS = 31
FR = 128
WIDE = 384
LANES = 128
PAIRS = HEADS * HEAD_DIM // LANES
WIDTH = HEADS * HEAD_DIM
EPS = 1e-05
NEG = -1e30
LOG2E = 1.4426950408889634
SCALE = HEAD_DIM ** (-0.5)
NX = 4
NC = 2
GROUP = NX * NC
TILES = PAIRS * 4
PIECE = TILES // GROUP
PART = PIECE // 2
MESH = pl.DeviceIdType.MESH


def lanes_of(p):
    return pl.ds(pl.multiple_of(p * LANES, LANES), LANES)


def dot_nt(a, b):
    return lax.dot_general(a, b, (((1,), (1,)), ((), ())), preferred_element_type=F32)


def dot_nn(a, b):
    return lax.dot_general(a, b, (((1,), (0,)), ((), ())), preferred_element_type=F32)


def kernel(
    nz,
    ny,
    q_hbm,
    k_hbm,
    v_hbm,
    cot_hbm,
    seg_hbm,
    gain_hbm,
    ker_hbm,
    bias_hbm,
    conv_hbm,
    dq_hbm,
    dk_hbm,
    dv_hbm,
    sums_hbm,
    gain_ref,
    ker_ref,
    bias_ref,
    kbuf,
    vbuf,
    qbuf,
    cotbuf,
    segbuf,
    segc,
    maskb,
    cm,
    wb,
    bb,
    gb,
    pbuf,
    ctx,
    ctxt,
    xbuf,
    gbuf,
    meanb,
    invb,
    acc1,
    acc2,
    xsend,
    xrecv,
    gsend,
    grecv,
    kg,
    xm,
    dkv_own,
    gnorm,
    maskn,
    lse,
    lse_n,
    delta,
    delta_n,
    q_n,
    dc_buf,
    dc_n,
    dq_buf,
    conv_buf,
    red,
    r_in,
    za_in,
    yb_in,
    ya_in,
    zb_in,
    sums,
    lsem,
    osem,
    kv_s,
    kv_r,
    xs,
    xr,
    gs,
    gr,
    l_s,
    l_r,
    q_s,
    q_r,
    t_s,
    t_r,
    c_s,
    c_r,
    r_s,
    r_r,
    z_s,
    z_r,
    y_s,
    y_r,
    a_s,
    a_r,
):
    nseq = nz * NX * NC
    me = lax.axis_index("seq")
    row = lax.axis_index("dp")
    right = lax.rem(me + 1, nseq)
    left = lax.rem(me + nseq - 1, nseq)
    mg = lax.rem(me, GROUP)
    mz = me // GROUP

    def seq_dev(s):
        return (row, s)

    def g_dev(k):
        return seq_dev(mz * GROUP + lax.rem(mg + k, GROUP))

    def z_dev(k):
        return seq_dev(lax.rem(mz + k, nz) * GROUP + mg)

    def y_dev(k):
        return (lax.rem(row + k, ny), me)

    far_g = [4, 3, 5, 2, 6, 1, 7]
    far_z = sorted(range(1, nz), key=lambda k: -min(k, nz - k))
    far_y = sorted(range(1, ny), key=lambda k: -min(k, ny - k))
    sides = (seq_dev(right), seq_dev(left))

    def remote(src, dst, s, r, dev):
        return pltpu.make_async_remote_copy(
            src_ref=src, dst_ref=dst, send_sem=s, recv_sem=r, device_id=dev, device_id_type=MESH
        )

    own = pl.ds(FR, FR)
    locals_ = [
        pltpu.make_async_copy(k_hbm, kbuf.at[own, :], lsem.at[0]),
        pltpu.make_async_copy(v_hbm, vbuf.at[own, :], lsem.at[1]),
        pltpu.make_async_copy(q_hbm, qbuf, lsem.at[2]),
        pltpu.make_async_copy(cot_hbm, cotbuf, lsem.at[3]),
    ]
    for j, blk in enumerate((left, me, right)):
        locals_.append(
            pltpu.make_async_copy(
                seg_hbm.at[:, pl.ds(pl.multiple_of(blk * FR, FR), FR)],
                segbuf.at[j],
                lsem.at[4 + j],
            )
        )
    locals_.append(pltpu.make_async_copy(gain_hbm, gain_ref, lsem.at[7]))
    locals_.append(pltpu.make_async_copy(ker_hbm, ker_ref, lsem.at[8]))
    locals_.append(pltpu.make_async_copy(bias_hbm, bias_ref, lsem.at[9]))

    barrier = pltpu.get_barrier_semaphore()
    partners = list(sides)
    partners += [g_dev(k) for k in far_g]
    partners += [z_dev(k) for k in far_z]
    partners += [y_dev(k) for k in far_y]
    for dev in partners:
        pl.semaphore_signal(barrier, inc=1, device_id=dev, device_id_type=MESH)
    for copy in locals_[::-1]:
        copy.start()
    pl.semaphore_wait(barrier, len(partners))

    def kv_copy(side, kv, p):
        src = (k_hbm, v_hbm)[kv]
        dst = (kbuf, vbuf)[kv]
        return remote(
            src.at[:, lanes_of(p)],
            dst.at[pl.ds(pl.multiple_of(2 * FR * side, FR), FR), lanes_of(p)],
            kv_s,
            kv_r.at[side, kv, p],
            seq_dev(lax.rem(me + nseq + 1 - 2 * side, nseq)),
        )

    off_chip = 1 - lax.rem(me, NC)
    for side in (off_chip, 1 - off_chip):

        @pl.loop(0, PAIRS)
        def _(p):
            for kv in range(2):
                kv_copy(side, kv, p).start()

    zero = jnp.zeros((FR, LANES), F32)
    acc1[...] = zero
    for j in range(3):
        locals_[4 + j].wait()
    own_row = segbuf[1]
    for j in range(3):
        col = jnp.broadcast_to(segbuf[j], (FR, LANES)).T
        segc[pl.ds(j * FR, FR), :] = col
        maskb[pl.ds(j * FR, FR), :] = jnp.where(col == own_row, 0.0, NEG)
    own_col = segc[pl.ds(FR, FR), :]
    for side in range(2):
        maskn[side] = jnp.where(own_col == segbuf[2 * side], 0.0, NEG)
    for t in range(TAPS):
        cm[t] = jnp.where(segc[pl.ds(FR + t - 15, FR), :] == own_col, 1.0, 0.0)

    for j in range(7, 10):
        locals_[j].wait()

    @pl.loop(0, PAIRS)
    def _(c):
        for t in range(TAPS):
            wb[c, t] = jnp.broadcast_to(ker_ref[t : t + 1, lanes_of(c)], (8, LANES))
        bb[c] = jnp.broadcast_to(bias_ref[lanes_of(c)].reshape(1, LANES), (8, LANES))
        gb[c] = jnp.broadcast_to(gain_ref[lanes_of(c)].reshape(1, LANES), (8, LANES))
        kg[c] = jnp.zeros_like(kg[c])

    for j in range(3):
        locals_[j].wait()
    low = lax.broadcasted_iota(jnp.int32, (FR, LANES), 1) < HEAD_DIM

    def diag(block):
        zero = jnp.zeros_like(block)
        return jnp.concatenate([jnp.where(low, block, zero), jnp.where(low, zero, block)], 0)

    def pick(block):
        return jnp.concatenate([block[:HEAD_DIM, :LANES], block[HEAD_DIM:, LANES:]], 0)

    @pl.loop(0, PAIRS)
    def _(p):
        for kv in range(2):
            for side in range(2):
                kv_copy(side, kv, p).wait_recv()
        key = kbuf[:, lanes_of(p)]
        val = vbuf[:, lanes_of(p)]
        qd = diag(qbuf[:, lanes_of(p)])
        mask = maskb[...]
        s = dot_nt(key, qd) * (SCALE * LOG2E) + jnp.concatenate([mask, mask], 1)
        top = jnp.max(s, 0, keepdims=True)
        e = jnp.exp2(s - top)
        total = jnp.sum(e, 0, keepdims=True)
        inv = 1.0 / total
        lse[p] = top + jnp.log(total) * LOG2E
        prob = (e * inv).astype(BF)
        pbuf[p] = prob
        ct = pick(dot_nn(val.T, prob)).astype(BF).astype(F32)
        ctxt[p] = ct
        ct = ct.T
        ctx[p] = ct
        acc1[...] = acc1[...] + ct

    mean = jnp.broadcast_to(jnp.sum(acc1[...], 1, keepdims=True) * (1.0 / WIDTH), (FR, LANES))
    meanb[...] = mean

    def square(c, a):
        d = ctx[c] - meanb[...]
        return a + d * d

    total = lax.fori_loop(0, PAIRS, square, zero)
    var = jnp.sum(total, 1, keepdims=True) * (1.0 / WIDTH)
    invb[...] = jnp.broadcast_to(lax.rsqrt(var + EPS), (FR, LANES))

    @pl.loop(0, PAIRS)
    def _(c):
        normed = (ctx[c] - meanb[...]) * invb[...]
        ctx[c] = normed
        x = (normed.reshape(16, 8, LANES) * gb[c][None]).reshape(FR, LANES).astype(BF)
        xsend[1, c] = x[:16]
        xsend[0, c] = x[FR - 16 :]
        xbuf[c, pl.ds(16, FR), :] = x.astype(F32)

    def x_copy(side):
        return remote(xsend.at[side], xrecv.at[side], xs.at[side], xr.at[side], sides[side])

    def g_copy(side):
        return remote(gsend.at[side], grecv.at[side], gs.at[side], gr.at[side], sides[side])

    def l_copy(side):
        return remote(lse, lse_n.at[side], l_s.at[side], l_r.at[side], sides[side])

    def q_copy(side):
        return remote(q_hbm, q_n.at[side], q_s.at[side], q_r.at[side], sides[side])

    def t_copy(side):
        return remote(delta, delta_n.at[side], t_s.at[side], t_r.at[side], sides[side])

    def c_copy(side, chunk):
        at = pl.ds(chunk * 3 * LANES, 3 * LANES)
        return remote(
            dc_buf.at[:, at], dc_n.at[side, :, at], c_s, c_r.at[side, chunk], sides[side]
        )

    for side in range(2):
        x_copy(side).start()
    for side in range(2):
        l_copy(side).start()
    for side in range(2):
        q_copy(side).start()
    locals_[3].wait()

    def rows_of(ref, c, base, count):
        return ref.at[c] if base is None else ref.at[c, pl.ds(base, count), :]

    def conv_group(chunks, base, tiles):
        xs_ = [rows_of(xbuf, c, base, 64) for c in chunks]
        count = len(tiles)
        acc = [[bb[c] for _ in tiles] for c in chunks]
        for t in range(TAPS):
            mt = rows_of(cm, t, base, 32)
            ms = [mt[pl.ds(r, 8), :] for r in tiles]
            for j, c in enumerate(chunks):
                w = wb[c, t]
                for i, r in enumerate(tiles):
                    x = ms[i] * xs_[j][pl.ds(r + t + 1, 8), :]
                    xm[t, j * count + i] = x
                    acc[j][i] = acc[j][i] + w * x
        gr_ = []
        for j, c in enumerate(chunks):
            gr_.append([])
            for i, r in enumerate(tiles):
                a = acc[j][i]
                sig = 1.0 / (1.0 + jnp.exp(-a))
                acc[j][i] = a * sig
                gr_[j].append(sig * (1.0 + a * (1.0 - sig)))
        for j, c in enumerate(chunks):
            for h in range(0, len(tiles), 2):
                at = tiles[h] if base is None else base + tiles[h]
                out = jnp.concatenate(acc[j][h : h + 2], 0).astype(BF)
                conv_buf[pl.ds(at, 16), lanes_of(c)] = out
                g = jnp.concatenate(gr_[j][h : h + 2], 0)
                g = (g * cotbuf[pl.ds(at, 16), lanes_of(c)].astype(F32)).astype(BF)
                if base is None and h == 0:
                    gsend[1, c] = g
                elif base is None:
                    gsend[0, c] = g
                g = g.astype(F32)
                gbuf[c, pl.ds(at + 16, 16), :] = g
                gr_[j][h] = g[:8]
                gr_[j][h + 1] = g[8:]
            kg[c, TAPS] = kg[c, TAPS] + functools.reduce(jnp.add, gr_[j])
        for t in range(TAPS):
            for j, c in enumerate(chunks):
                terms = [gr_[j][i] * xm[t, j * count + i] for i in range(count)]
                kg[c, t] = kg[c, t] + functools.reduce(jnp.add, terms)

    edges = [0, 8, FR - 16, FR - 8]
    tap_row = lax.broadcasted_iota(jnp.int32, (TAPS + 1, TAPS * 8 + 8), 0)
    sub_row = lax.broadcasted_iota(jnp.int32, (TAPS + 1, TAPS * 8 + 8), 1) // 8
    rows8 = jnp.where(tap_row == sub_row, 1.0, 0.0).astype(BF)

    @pl.loop(0, PAIRS // 2)
    def _(cc):
        @pl.loop(0, 3)
        def _(rr):
            conv_group([2 * cc, 2 * cc + 1], pl.multiple_of(rr * 32 + 16, 16), [0, 8, 16, 24])

    for side in range(2):
        x_copy(side).wait_recv()

    @pl.loop(0, PAIRS // 2)
    def _(cc):
        for c in (2 * cc, 2 * cc + 1):
            xbuf[c, pl.ds(0, 16), :] = xrecv[0, c].astype(F32)
            xbuf[c, pl.ds(FR + 16, 16), :] = xrecv[1, c].astype(F32)
        conv_group([2 * cc, 2 * cc + 1], None, edges)
        for c in (2 * cc, 2 * cc + 1):
            whole = kg[c].reshape(TAPS * 8 + 8, LANES)
            high = whole.astype(BF)
            low_part = (whole - high.astype(F32)).astype(BF)
            total = dot_nn(rows8, high) + dot_nn(rows8, low_part)
            for rg in range(4):
                red[rg * PAIRS + c] = total[rg * 8 : rg * 8 + 8].astype(BF)

    for side in range(2):
        g_copy(side).start()

    mine = pl.ds(mg * PIECE, PIECE)

    def r_copy(k):
        to = lax.rem(mg + k, GROUP)
        return remote(
            red.at[pl.ds(to * PIECE, PIECE)], r_in.at[mg], r_s, r_r.at[k - 1], g_dev(k)
        )

    def z_copy(buf, j, k):
        return remote(buf.at[mz], buf.at[mz], z_s.at[j], z_r.at[j, k - 1], z_dev(k))

    def y_copy(buf, j, k):
        return remote(buf.at[row], buf.at[row], y_s.at[j], y_r.at[j, k - 1], y_dev(k))

    def a_copy(k):
        return remote(sums.at[mine], sums.at[mine], a_s, a_r.at[k - 1], g_dev(k))

    def add_up(buf, count):
        return functools.reduce(jnp.add, [buf[i].astype(F32) for i in range(count)])

    for k in far_g:
        r_copy(k).start()
    r_in[mg] = red[mine]

    conv_done = pltpu.make_async_copy(conv_buf, conv_hbm, osem.at[0])
    conv_done.start()

    def in_group(chunks, base, tiles):
        gs_ = [rows_of(gbuf, c, base, 64) for c in chunks]
        acc = [[None for _ in tiles] for c in chunks]
        for u in range(TAPS):
            mt = rows_of(cm, u, base, 32)
            ms = [mt[pl.ds(r, 8), :] for r in tiles]
            for j, c in enumerate(chunks):
                w = wb[c, TAPS - 1 - u]
                for i, r in enumerate(tiles):
                    term = w * (ms[i] * gs_[j][pl.ds(r + u + 1, 8), :])
                    acc[j][i] = term if u == 0 else acc[j][i] + term
        for i, r in enumerate(tiles):
            at = pl.ds(r if base is None else base + r, 8)
            s1 = acc1[at, :]
            s2 = acc2[at, :]
            for j, c in enumerate(chunks):
                g = acc[j][i] * gb[c]
                gnorm[c, at, :] = g
                s1 = s1 + g
                s2 = s2 + g * ctx[c, at, :]
            acc1[at, :] = s1
            acc2[at, :] = s2

    acc1[...] = zero
    acc2[...] = zero

    @pl.loop(0, PAIRS // 2)
    def _(cc):
        @pl.loop(0, 3)
        def _(rr):
            in_group([2 * cc, 2 * cc + 1], pl.multiple_of(rr * 32 + 16, 16), [0, 8, 16, 24])

    for side in range(2):
        g_copy(side).wait_recv()

    @pl.loop(0, PAIRS // 2)
    def _(cc):
        for c in (2 * cc, 2 * cc + 1):
            gbuf[c, pl.ds(0, 16), :] = grecv[0, c].astype(F32)
            gbuf[c, pl.ds(FR + 16, 16), :] = grecv[1, c].astype(F32)
        in_group([2 * cc, 2 * cc + 1], None, edges)

    for k in far_g:
        r_copy(k).wait_recv()
    part = add_up(r_in, GROUP).astype(BF)
    za_in[mz] = part[:PART]
    yb_in[row] = part[PART:]
    for k in far_z:
        z_copy(za_in, 0, k).start()
    for k in far_y:
        y_copy(yb_in, 0, k).start()

    acc1[...] = jnp.broadcast_to(jnp.sum(acc1[...], 1, keepdims=True) * (1.0 / WIDTH), (FR, LANES))
    acc2[...] = jnp.broadcast_to(jnp.sum(acc2[...], 1, keepdims=True) * (1.0 / WIDTH), (FR, LANES))

    @pl.loop(0, PAIRS)
    def _(p):
        dc = (gnorm[p] - acc1[...] - ctx[p] * acc2[...]) * invb[...]
        dc = dc.astype(BF)
        dc_buf[:, lanes_of(p)] = dc
        prod = dc.astype(F32).T * ctxt[p]
        delta[p] = jnp.concatenate(
            [
                jnp.sum(prod[:HEAD_DIM], 0, keepdims=True),
                jnp.sum(prod[HEAD_DIM:], 0, keepdims=True),
            ],
            1,
        )

    for side in range(2):
        t_copy(side).start()
    for chunk in range(4):
        for side in range(2):
            c_copy(side, chunk).start()

    def back(p):
        key = kbuf[:, lanes_of(p)]
        val = vbuf[:, lanes_of(p)]
        dcd = diag(dc_buf[:, lanes_of(p)])
        qd = diag(qbuf[:, lanes_of(p)])
        prob = pbuf[p]
        dp = dot_nt(val, dcd)
        ds = (prob.astype(F32) * ((dp - delta[p]) * SCALE)).astype(BF)
        dkv_own[0, p] = dot_nn(ds[FR : 2 * FR], qd)
        dkv_own[1, p] = dot_nn(prob[FR : 2 * FR], dcd)
        dq_buf[:, lanes_of(p)] = pick(dot_nn(key.T, ds)).T.astype(BF)

    def back_near(p):
        key = kbuf[pl.ds(FR, FR), lanes_of(p)]
        val = vbuf[pl.ds(FR, FR), lanes_of(p)]
        qd = jnp.concatenate([diag(q_n[side, :, lanes_of(p)]) for side in range(2)], 0)
        dcd = jnp.concatenate([diag(dc_n[side, :, lanes_of(p)]) for side in range(2)], 0)
        shift = jnp.concatenate([lse_n[side, p] for side in range(2)], 1)
        dlt = jnp.concatenate([delta_n[side, p] for side in range(2)], 1)
        mask = jnp.concatenate([maskn[0], maskn[0], maskn[1], maskn[1]], 1)
        prob = jnp.exp2(dot_nt(key, qd) * (SCALE * LOG2E) + (mask - shift))
        ds = (prob * ((dot_nt(val, dcd) - dlt) * SCALE)).astype(BF)
        dk = dkv_own[0, p] + dot_nn(ds, qd)
        dv = dkv_own[1, p] + dot_nn(prob.astype(BF), dcd)
        kbuf[pl.ds(FR, FR), lanes_of(p)] = dk.astype(BF)
        vbuf[pl.ds(FR, FR), lanes_of(p)] = dv.astype(BF)

    pl.loop(0, 7)(back)

    for k in far_z:
        z_copy(za_in, 0, k).wait_recv()
    for k in far_y:
        y_copy(yb_in, 0, k).wait_recv()
    ya_in[row] = add_up(za_in, nz).astype(BF)
    zb_in[mz] = add_up(yb_in, ny).astype(BF)
    for k in far_y:
        y_copy(ya_in, 1, k).start()
    for k in far_z:
        z_copy(zb_in, 1, k).start()

    pl.loop(7, PAIRS)(back)

    dq_done = pltpu.make_async_copy(dq_buf, dq_hbm, osem.at[1])
    dq_done.start()

    for side in range(2):
        l_copy(side).wait_recv()
        q_copy(side).wait_recv()
        t_copy(side).wait_recv()
    for chunk in range(2):
        for side in range(2):
            c_copy(side, chunk).wait_recv()
    pl.loop(0, 5)(back_near)

    for k in far_y:
        y_copy(ya_in, 1, k).wait_recv()
    for k in far_z:
        z_copy(zb_in, 1, k).wait_recv()
    sums[pl.ds(mg * PIECE, PART)] = add_up(ya_in, ny).astype(BF)
    sums[pl.ds(mg * PIECE + PART, PART)] = add_up(zb_in, nz).astype(BF)
    for k in far_g:
        a_copy(k).start()

    for chunk in range(2, 4):
        for side in range(2):
            c_copy(side, chunk).wait_recv()
    pl.loop(5, PAIRS)(back_near)

    dk_done = pltpu.make_async_copy(kbuf.at[own, :], dk_hbm, osem.at[2])
    dv_done = pltpu.make_async_copy(vbuf.at[own, :], dv_hbm, osem.at[3])
    dk_done.start()
    dv_done.start()

    for k in far_g:
        a_copy(k).wait_recv()
    sums_done = pltpu.make_async_copy(sums, sums_hbm, osem.at[4])
    sums_done.start()

    def sent(buf, sem):
        remote(buf, buf, sem, sem, sides[0]).wait_send()

    sent(pbuf.at[pl.ds(0, 8)], kv_s)
    sent(pbuf.at[pl.ds(0, 4)], c_s)
    for side in range(2):
        x_copy(side).wait_send()
        g_copy(side).wait_send()
        l_copy(side).wait_send()
        q_copy(side).wait_send()
        t_copy(side).wait_send()
    others = pl.ds(0, GROUP - 1)
    sent(r_in.at[others], r_s)
    sent(r_in.at[others], a_s)
    for j in range(2):
        sent(za_in.at[pl.ds(0, nz - 1)], z_s.at[j])
        sent(yb_in.at[pl.ds(0, ny - 1)], y_s.at[j])
    sums_done.wait()
    conv_done.wait()
    dq_done.wait()
    dk_done.wait()
    dv_done.wait()


def finish(
    factor,
    conv_in,
    dq_in,
    dk_in,
    dv_in,
    sums_in,
    gain_hbm,
    ker_hbm,
    conv_out,
    dq_out,
    dk_out,
    dv_out,
    gain_out,
    ker_out,
    bias_out,
    gain_ref,
    ker_ref,
    sem,
):
    loads = [
        pltpu.make_async_copy(gain_hbm, gain_ref, sem.at[4]),
        pltpu.make_async_copy(ker_hbm, ker_ref, sem.at[5]),
    ]
    for copy in loads:
        copy.start()
    copies = [
        pltpu.make_async_copy(a, b, sem.at[i])
        for i, (a, b) in enumerate(
            ((conv_in, conv_out), (dq_in, dq_out), (dk_in, dk_out), (dv_in, dv_out))
        )
    ]
    for copy in copies:
        copy.start()
    for copy in loads:
        copy.wait()
    for c in range(PAIRS):
        at = slice(c * LANES, (c + 1) * LANES)
        gsum = jnp.zeros((8, LANES), F32)
        for rg in range(4):
            tile = sums_in[rg * PAIRS + c].astype(F32) * factor
            if rg < 3:
                ker_out[rg * 8 : rg * 8 + 8, at] = tile
                gsum = gsum + tile * ker_ref[rg * 8 : rg * 8 + 8, at]
            else:
                ker_out[24:31, at] = tile[:7]
                bias_out[at] = tile[7]
                gsum = gsum + jnp.concatenate(
                    [tile[:7] * ker_ref[24:31, at], jnp.zeros((1, LANES), F32)], 0
                )
        gain_out[at] = jnp.sum(gsum, 0) / gain_ref[at]
    for copy in copies:
        copy.wait()


def per_device(nz, ny, queries, keys, values, segment_ids, norm_gain, conv_kernel, conv_bias, cot):
    dma = pltpu.SemaphoreType.DMA
    vmem = pltpu.VMEM
    any_ = pl.BlockSpec(memory_space=pl.ANY)
    whole = pl.BlockSpec(memory_space=pltpu.VMEM)
    row = jax.ShapeDtypeStruct((FR, WIDTH), BF)
    in_hbm = functools.partial(pltpu.with_memory_space_constraint, memory_space=pltpu.HBM)
    rows = [in_hbm(a[0]) for a in (queries, keys, values, cot)]
    segment_ids, gain_in, ker_in, bias_in = map(
        in_hbm, (segment_ids, norm_gain, conv_kernel, conv_bias)
    )
    outs = pl.pallas_call(
        functools.partial(kernel, nz, ny),
        out_shape=(
            row,
            row,
            row,
            row,
            jax.ShapeDtypeStruct((TILES, 8, LANES), BF),
        ),
        in_specs=[any_] * 8,
        out_specs=(any_,) * 5,
        scratch_shapes=[
            vmem((WIDTH,), F32),
            vmem((TAPS, WIDTH), F32),
            vmem((WIDTH,), F32),
            vmem((WIDE, WIDTH), BF),
            vmem((WIDE, WIDTH), BF),
            vmem((FR, WIDTH), BF),
            vmem((FR, WIDTH), BF),
            vmem((3, 1, FR), jnp.int32),
            vmem((WIDE, LANES), jnp.int32),
            vmem((WIDE, LANES), F32),
            vmem((TAPS, FR, LANES), F32),
            vmem((PAIRS, TAPS, 8, LANES), F32),
            vmem((PAIRS, 8, LANES), F32),
            vmem((PAIRS, 8, LANES), F32),
            vmem((PAIRS, WIDE, 2 * LANES), BF),
            vmem((PAIRS, FR, LANES), F32),
            vmem((PAIRS, FR, LANES), F32),
            vmem((PAIRS, FR + 32, LANES), F32),
            vmem((PAIRS, FR + 32, LANES), F32),
            vmem((FR, LANES), F32),
            vmem((FR, LANES), F32),
            vmem((FR, LANES), F32),
            vmem((FR, LANES), F32),
            vmem((2, PAIRS, 16, LANES), BF),
            vmem((2, PAIRS, 16, LANES), BF),
            vmem((2, PAIRS, 16, LANES), BF),
            vmem((2, PAIRS, 16, LANES), BF),
            vmem((PAIRS, 32, 8, LANES), F32),
            vmem((TAPS, 8, 8, LANES), F32),
            vmem((2, PAIRS, FR, LANES), F32),
            vmem((PAIRS, FR, LANES), F32),
            vmem((2, FR, LANES), F32),
            vmem((PAIRS, 1, 2 * LANES), F32),
            vmem((2, PAIRS, 1, 2 * LANES), F32),
            vmem((PAIRS, 1, 2 * LANES), F32),
            vmem((2, PAIRS, 1, 2 * LANES), F32),
            vmem((2, FR, WIDTH), BF),
            vmem((FR, WIDTH), BF),
            vmem((2, FR, WIDTH), BF),
            vmem((FR, WIDTH), BF),
            vmem((FR, WIDTH), BF),
            vmem((TILES, 8, LANES), BF),
            vmem((GROUP, PIECE, 8, LANES), BF),
            vmem((nz, PART, 8, LANES), BF),
            vmem((ny, PART, 8, LANES), BF),
            vmem((ny, PART, 8, LANES), BF),
            vmem((nz, PART, 8, LANES), BF),
            vmem((TILES, 8, LANES), BF),
            dma((10,)),
            dma((5,)),
            dma,
            dma((2, 2, PAIRS)),
            dma((2,)),
            dma((2,)),
            dma((2,)),
            dma((2,)),
            dma((2,)),
            dma((2,)),
            dma((2,)),
            dma((2,)),
            dma((2,)),
            dma((2,)),
            dma,
            dma((2, 4)),
            dma,
            dma((GROUP - 1,)),
            dma((2,)),
            dma((2, nz - 1)),
            dma((2,)),
            dma((2, ny - 1)),
            dma,
            dma((GROUP - 1,)),
        ],
        compiler_params=pltpu.CompilerParams(
            collective_id=0, has_side_effects=True, vmem_limit_bytes=36 * 1024 * 1024
        ),
    )(
        *rows,
        segment_ids,
        gain_in,
        ker_in,
        bias_in,
    )
    factor = (ny * nz * GROUP * FR) ** (-0.5)
    vec = jax.ShapeDtypeStruct((WIDTH,), F32)
    conv_out, dq, dk, dv, gain, ker, bias = pl.pallas_call(
        functools.partial(finish, factor),
        out_shape=(row, row, row, row, vec, jax.ShapeDtypeStruct((TAPS, WIDTH), F32), vec),
        in_specs=[any_] * 4 + [whole] + [any_] * 2,
        out_specs=(any_,) * 4 + (whole,) * 3,
        scratch_shapes=[vmem((WIDTH,), F32), vmem((TAPS, WIDTH), F32), dma((6,))],
        compiler_params=pltpu.CompilerParams(vmem_limit_bytes=4 * 1024 * 1024),
    )(*outs, gain_in, ker_in)
    return (conv_out[None], dq[None], dk[None], dv[None], gain, ker, bias)


def solution(mesh):
    rows = P("dp", "seq", None)
    nz = mesh.shape["seq"] // (NX * NC)
    return jax.shard_map(
        functools.partial(per_device, nz, mesh.shape["dp"]),
        mesh=mesh,
        in_specs=(rows, rows, rows, P("dp", None), P(), P(), P(), rows),
        out_specs=(rows, rows, rows, rows, P(), P(), P()),
        check_vma=False,
    )
```

```python
import functools

import jax
import jax.numpy as jnp
from jax import lax
from jax.experimental import pallas as pl
from jax.experimental.pallas import tpu as pltpu
from jax.sharding import PartitionSpec as P

BF = jnp.bfloat16
F32 = jnp.float32
HEADS = 24
HEAD_DIM = 64
TAPS = 31
FR = 128
WIDE = 384
LANES = 128
PAIRS = HEADS * HEAD_DIM // LANES
WIDTH = HEADS * HEAD_DIM
EPS = 1e-05
NEG = -1e30
LOG2E = 1.4426950408889634
SCALE = HEAD_DIM ** (-0.5)
NX = 4
NC = 2
GROUP = NX * NC
TILES = PAIRS * 4
PIECE = TILES // GROUP
PART = PIECE // 2
MESH = pl.DeviceIdType.MESH


def lanes_of(p):
    return pl.ds(pl.multiple_of(p * LANES, LANES), LANES)


def dot_nt(a, b):
    return lax.dot_general(a, b, (((1,), (1,)), ((), ())), preferred_element_type=F32)


def dot_nn(a, b):
    return lax.dot_general(a, b, (((1,), (0,)), ((), ())), preferred_element_type=F32)


def kernel(
    nz,
    ny,
    q_hbm,
    k_hbm,
    v_hbm,
    cot_hbm,
    seg_hbm,
    gain_hbm,
    ker_hbm,
    bias_hbm,
    conv_hbm,
    dq_hbm,
    dk_hbm,
    dv_hbm,
    sums_hbm,
    gain_ref,
    ker_ref,
    bias_ref,
    kbuf,
    vbuf,
    qbuf,
    cotbuf,
    segbuf,
    segc,
    maskb,
    cm,
    wb,
    bb,
    gb,
    pbuf,
    ctx,
    ctxt,
    xbuf,
    gbuf,
    meanb,
    invb,
    acc1,
    acc2,
    xsend,
    xrecv,
    gsend,
    grecv,
    kg,
    xm,
    dkv_own,
    gnorm,
    maskn,
    lse,
    lse_n,
    delta,
    delta_n,
    q_n,
    dc_buf,
    dc_n,
    dq_buf,
    conv_buf,
    red,
    r_in,
    za_in,
    yb_in,
    ya_in,
    zb_in,
    sums,
    lsem,
    osem,
    kv_s,
    kv_r,
    xs,
    xr,
    gs,
    gr,
    l_s,
    l_r,
    q_s,
    q_r,
    t_s,
    t_r,
    c_s,
    c_r,
    r_s,
    r_r,
    z_s,
    z_r,
    y_s,
    y_r,
    a_s,
    a_r,
):
    nseq = nz * NX * NC
    me = lax.axis_index("seq")
    row = lax.axis_index("dp")
    right = lax.rem(me + 1, nseq)
    left = lax.rem(me + nseq - 1, nseq)
    mg = lax.rem(me, GROUP)
    mz = me // GROUP

    def seq_dev(s):
        return (row, s)

    def g_dev(k):
        return seq_dev(mz * GROUP + lax.rem(mg + k, GROUP))

    def z_dev(k):
        return seq_dev(lax.rem(mz + k, nz) * GROUP + mg)

    def y_dev(k):
        return (lax.rem(row + k, ny), me)

    far_g = [4, 3, 5, 2, 6, 1, 7]
    far_z = sorted(range(1, nz), key=lambda k: -min(k, nz - k))
    far_y = sorted(range(1, ny), key=lambda k: -min(k, ny - k))
    sides = (seq_dev(right), seq_dev(left))
    has_right = me < nseq - 1
    has_left = me > 0
    sends = (has_right, has_left)
    takes = (has_left, has_right)

    def remote(src, dst, s, r, dev):
        return pltpu.make_async_remote_copy(
            src_ref=src, dst_ref=dst, send_sem=s, recv_sem=r, device_id=dev, device_id_type=MESH
        )

    own = pl.ds(FR, FR)
    locals_ = [
        pltpu.make_async_copy(k_hbm, kbuf.at[own, :], lsem.at[0]),
        pltpu.make_async_copy(v_hbm, vbuf.at[own, :], lsem.at[1]),
        pltpu.make_async_copy(q_hbm, qbuf, lsem.at[2]),
        pltpu.make_async_copy(cot_hbm, cotbuf, lsem.at[3]),
    ]
    for j, blk in enumerate((left, me, right)):
        locals_.append(
            pltpu.make_async_copy(
                seg_hbm.at[:, pl.ds(pl.multiple_of(blk * FR, FR), FR)],
                segbuf.at[j],
                lsem.at[4 + j],
            )
        )
    locals_.append(pltpu.make_async_copy(gain_hbm, gain_ref, lsem.at[7]))
    locals_.append(pltpu.make_async_copy(ker_hbm, ker_ref, lsem.at[8]))
    locals_.append(pltpu.make_async_copy(bias_hbm, bias_ref, lsem.at[9]))

    barrier = pltpu.get_barrier_semaphore()
    partners = list(sides)
    partners += [g_dev(k) for k in far_g]
    partners += [z_dev(k) for k in far_z]
    partners += [y_dev(k) for k in far_y]
    for dev in partners:
        pl.semaphore_signal(barrier, inc=1, device_id=dev, device_id_type=MESH)
    for copy in locals_[::-1]:
        copy.start()
    pl.semaphore_wait(barrier, len(partners))

    def kv_copy(side, kv, p):
        src = (k_hbm, v_hbm)[kv]
        dst = (kbuf, vbuf)[kv]
        return remote(
            src.at[:, lanes_of(p)],
            dst.at[pl.ds(2 * FR * side, FR), lanes_of(p)],
            kv_s.at[side],
            kv_r.at[side, kv, p],
            sides[side],
        )

    for side in range(2):

        @pl.when(sends[side])
        def _(side=side):
            @pl.loop(0, PAIRS)
            def _(p):
                for kv in range(2):
                    kv_copy(side, kv, p).start()

        @pl.when(jnp.logical_not(takes[side]))
        def _(side=side):
            rows = pl.ds(2 * FR * side, FR)
            kbuf[rows, :] = jnp.zeros((FR, WIDTH), BF)
            vbuf[rows, :] = jnp.zeros((FR, WIDTH), BF)
            q_n[side] = jnp.zeros((FR, WIDTH), BF)
            dc_n[side] = jnp.zeros((FR, WIDTH), BF)
            lse_n[side] = jnp.zeros((PAIRS, 1, 2 * LANES), F32)
            delta_n[side] = jnp.zeros((PAIRS, 1, 2 * LANES), F32)
            xrecv[side] = jnp.zeros((PAIRS, 16, LANES), BF)
            grecv[side] = jnp.zeros((PAIRS, 16, LANES), BF)

    zero = jnp.zeros((FR, LANES), F32)
    acc1[...] = zero
    for j in range(3):
        locals_[4 + j].wait()
    own_row = segbuf[1]
    for j in range(3):
        col = jnp.broadcast_to(segbuf[j], (FR, LANES)).T
        segc[pl.ds(j * FR, FR), :] = col
        maskb[pl.ds(j * FR, FR), :] = jnp.where(col == own_row, 0.0, NEG)
    own_col = segc[pl.ds(FR, FR), :]
    for side in range(2):
        maskn[side] = jnp.where(own_col == segbuf[2 * side], 0.0, NEG)
    for t in range(TAPS):
        cm[t] = jnp.where(segc[pl.ds(FR + t - 15, FR), :] == own_col, 1.0, 0.0)

    for j in range(7, 10):
        locals_[j].wait()

    @pl.loop(0, PAIRS)
    def _(c):
        for t in range(TAPS):
            wb[c, t] = jnp.broadcast_to(ker_ref[t : t + 1, lanes_of(c)], (8, LANES))
        bb[c] = jnp.broadcast_to(bias_ref[lanes_of(c)].reshape(1, LANES), (8, LANES))
        gb[c] = jnp.broadcast_to(gain_ref[lanes_of(c)].reshape(1, LANES), (8, LANES))
        kg[c] = jnp.zeros_like(kg[c])

    for j in range(3):
        locals_[j].wait()
    low = lax.broadcasted_iota(jnp.int32, (FR, LANES), 1) < HEAD_DIM

    def diag(block):
        zero = jnp.zeros_like(block)
        return jnp.concatenate([jnp.where(low, block, zero), jnp.where(low, zero, block)], 0)

    def pick(block):
        return jnp.concatenate([block[:HEAD_DIM, :LANES], block[HEAD_DIM:, LANES:]], 0)

    @pl.loop(0, PAIRS)
    def _(p):
        for side in range(2):

            @pl.when(takes[side])
            def _(side=side):
                for kv in range(2):
                    kv_copy(side, kv, p).wait_recv()

        key = kbuf[:, lanes_of(p)]
        val = vbuf[:, lanes_of(p)]
        qd = diag(qbuf[:, lanes_of(p)])
        mask = maskb[...]
        s = dot_nt(key, qd) * (SCALE * LOG2E) + jnp.concatenate([mask, mask], 1)
        top = jnp.max(s, 0, keepdims=True)
        e = jnp.exp2(s - top)
        total = jnp.sum(e, 0, keepdims=True)
        inv = 1.0 / total
        lse[p] = top + jnp.log(total) * LOG2E
        prob = (e * inv).astype(BF)
        pbuf[p] = prob
        ct = pick(dot_nn(val.T, prob)).astype(BF).astype(F32)
        ctxt[p] = ct
        ct = ct.T
        ctx[p] = ct
        acc1[...] = acc1[...] + ct

    mean = jnp.broadcast_to(jnp.sum(acc1[...], 1, keepdims=True) * (1.0 / WIDTH), (FR, LANES))
    meanb[...] = mean

    def square(c, a):
        d = ctx[c] - meanb[...]
        return a + d * d

    total = lax.fori_loop(0, PAIRS, square, zero)
    var = jnp.sum(total, 1, keepdims=True) * (1.0 / WIDTH)
    invb[...] = jnp.broadcast_to(lax.rsqrt(var + EPS), (FR, LANES))

    @pl.loop(0, PAIRS)
    def _(c):
        normed = (ctx[c] - meanb[...]) * invb[...]
        ctx[c] = normed
        x = (normed.reshape(16, 8, LANES) * gb[c][None]).reshape(FR, LANES).astype(BF)
        xsend[1, c] = x[:16]
        xsend[0, c] = x[FR - 16 :]
        xbuf[c, pl.ds(16, FR), :] = x.astype(F32)

    def x_copy(side):
        return remote(xsend.at[side], xrecv.at[side], xs.at[side], xr.at[side], sides[side])

    def g_copy(side):
        return remote(gsend.at[side], grecv.at[side], gs.at[side], gr.at[side], sides[side])

    def l_copy(side):
        return remote(lse, lse_n.at[side], l_s.at[side], l_r.at[side], sides[side])

    def q_copy(side):
        return remote(q_hbm, q_n.at[side], q_s.at[side], q_r.at[side], sides[side])

    def t_copy(side):
        return remote(delta, delta_n.at[side], t_s.at[side], t_r.at[side], sides[side])

    def c_copy(side, chunk):
        at = pl.ds(chunk * 3 * LANES, 3 * LANES)
        return remote(
            dc_buf.at[:, at], dc_n.at[side, :, at], c_s.at[side], c_r.at[side, chunk], sides[side]
        )

    def each(when, *what):
        for side in range(2):

            @pl.when(when[side])
            def _(side=side):
                for act in what:
                    act(side)

    each(
        sends,
        lambda side: x_copy(side).start(),
        lambda side: l_copy(side).start(),
        lambda side: q_copy(side).start(),
    )
    locals_[3].wait()

    def rows_of(ref, c, base, count):
        return ref.at[c] if base is None else ref.at[c, pl.ds(base, count), :]

    def conv_group(chunks, base, tiles):
        xs_ = [rows_of(xbuf, c, base, 64) for c in chunks]
        count = len(tiles)
        acc = [[bb[c] for _ in tiles] for c in chunks]
        for t in range(TAPS):
            mt = rows_of(cm, t, base, 32)
            ms = [mt[pl.ds(r, 8), :] for r in tiles]
            for j, c in enumerate(chunks):
                w = wb[c, t]
                for i, r in enumerate(tiles):
                    x = ms[i] * xs_[j][pl.ds(r + t + 1, 8), :]
                    xm[t, j * count + i] = x
                    acc[j][i] = acc[j][i] + w * x
        gr_ = []
        for j, c in enumerate(chunks):
            gr_.append([])
            for i, r in enumerate(tiles):
                a = acc[j][i]
                sig = 1.0 / (1.0 + jnp.exp(-a))
                acc[j][i] = a * sig
                gr_[j].append(sig * (1.0 + a * (1.0 - sig)))
        for j, c in enumerate(chunks):
            for h in range(0, len(tiles), 2):
                at = tiles[h] if base is None else base + tiles[h]
                out = jnp.concatenate(acc[j][h : h + 2], 0).astype(BF)
                conv_buf[pl.ds(at, 16), lanes_of(c)] = out
                g = jnp.concatenate(gr_[j][h : h + 2], 0)
                g = (g * cotbuf[pl.ds(at, 16), lanes_of(c)].astype(F32)).astype(BF)
                if base is None and h == 0:
                    gsend[1, c] = g
                elif base is None:
                    gsend[0, c] = g
                g = g.astype(F32)
                gbuf[c, pl.ds(at + 16, 16), :] = g
                gr_[j][h] = g[:8]
                gr_[j][h + 1] = g[8:]
            kg[c, TAPS] = kg[c, TAPS] + functools.reduce(jnp.add, gr_[j])
        for t in range(TAPS):
            for j, c in enumerate(chunks):
                terms = [gr_[j][i] * xm[t, j * count + i] for i in range(count)]
                kg[c, t] = kg[c, t] + functools.reduce(jnp.add, terms)

    edges = [0, 8, FR - 16, FR - 8]
    tap_row = lax.broadcasted_iota(jnp.int32, (TAPS + 1, TAPS * 8 + 8), 0)
    sub_row = lax.broadcasted_iota(jnp.int32, (TAPS + 1, TAPS * 8 + 8), 1) // 8
    rows8 = jnp.where(tap_row == sub_row, 1.0, 0.0).astype(BF)

    @pl.loop(0, PAIRS // 2)
    def _(cc):
        @pl.loop(0, 3)
        def _(rr):
            conv_group([2 * cc, 2 * cc + 1], pl.multiple_of(rr * 32 + 16, 16), [0, 8, 16, 24])

    each(takes, lambda side: x_copy(side).wait_recv())

    @pl.loop(0, PAIRS // 2)
    def _(cc):
        for c in (2 * cc, 2 * cc + 1):
            xbuf[c, pl.ds(0, 16), :] = xrecv[0, c].astype(F32)
            xbuf[c, pl.ds(FR + 16, 16), :] = xrecv[1, c].astype(F32)
        conv_group([2 * cc, 2 * cc + 1], None, edges)
        for c in (2 * cc, 2 * cc + 1):
            whole = kg[c].reshape(TAPS * 8 + 8, LANES)
            high = whole.astype(BF)
            low_part = (whole - high.astype(F32)).astype(BF)
            total = dot_nn(rows8, high) + dot_nn(rows8, low_part)
            for rg in range(4):
                red[rg * PAIRS + c] = total[rg * 8 : rg * 8 + 8].astype(BF)

    each(sends, lambda side: g_copy(side).start())

    mine = pl.ds(mg * PIECE, PIECE)

    def r_copy(k):
        to = lax.rem(mg + k, GROUP)
        return remote(
            red.at[pl.ds(to * PIECE, PIECE)], r_in.at[mg], r_s, r_r.at[k - 1], g_dev(k)
        )

    def z_copy(buf, j, k):
        return remote(buf.at[mz], buf.at[mz], z_s.at[j], z_r.at[j, k - 1], z_dev(k))

    def y_copy(buf, j, k):
        return remote(buf.at[row], buf.at[row], y_s.at[j], y_r.at[j, k - 1], y_dev(k))

    def a_copy(k):
        return remote(sums.at[mine], sums.at[mine], a_s, a_r.at[k - 1], g_dev(k))

    def add_up(buf, count):
        return functools.reduce(jnp.add, [buf[i].astype(F32) for i in range(count)])

    for k in far_g:
        r_copy(k).start()
    r_in[mg] = red[mine]

    conv_done = pltpu.make_async_copy(conv_buf, conv_hbm, osem.at[0])
    conv_done.start()

    def in_group(chunks, base, tiles):
        gs_ = [rows_of(gbuf, c, base, 64) for c in chunks]
        acc = [[None for _ in tiles] for c in chunks]
        for u in range(TAPS):
            mt = rows_of(cm, u, base, 32)
            ms = [mt[pl.ds(r, 8), :] for r in tiles]
            for j, c in enumerate(chunks):
                w = wb[c, TAPS - 1 - u]
                for i, r in enumerate(tiles):
                    term = w * (ms[i] * gs_[j][pl.ds(r + u + 1, 8), :])
                    acc[j][i] = term if u == 0 else acc[j][i] + term
        for i, r in enumerate(tiles):
            at = pl.ds(r if base is None else base + r, 8)
            s1 = acc1[at, :]
            s2 = acc2[at, :]
            for j, c in enumerate(chunks):
                g = acc[j][i] * gb[c]
                gnorm[c, at, :] = g
                s1 = s1 + g
                s2 = s2 + g * ctx[c, at, :]
            acc1[at, :] = s1
            acc2[at, :] = s2

    acc1[...] = zero
    acc2[...] = zero

    @pl.loop(0, PAIRS // 2)
    def _(cc):
        @pl.loop(0, 3)
        def _(rr):
            in_group([2 * cc, 2 * cc + 1], pl.multiple_of(rr * 32 + 16, 16), [0, 8, 16, 24])

    each(takes, lambda side: g_copy(side).wait_recv())

    @pl.loop(0, PAIRS // 2)
    def _(cc):
        for c in (2 * cc, 2 * cc + 1):
            gbuf[c, pl.ds(0, 16), :] = grecv[0, c].astype(F32)
            gbuf[c, pl.ds(FR + 16, 16), :] = grecv[1, c].astype(F32)
        in_group([2 * cc, 2 * cc + 1], None, edges)

    for k in far_g:
        r_copy(k).wait_recv()
    part = add_up(r_in, GROUP).astype(BF)
    za_in[mz] = part[:PART]
    yb_in[row] = part[PART:]
    for k in far_z:
        z_copy(za_in, 0, k).start()
    for k in far_y:
        y_copy(yb_in, 0, k).start()

    acc1[...] = jnp.broadcast_to(jnp.sum(acc1[...], 1, keepdims=True) * (1.0 / WIDTH), (FR, LANES))
    acc2[...] = jnp.broadcast_to(jnp.sum(acc2[...], 1, keepdims=True) * (1.0 / WIDTH), (FR, LANES))

    @pl.loop(0, PAIRS)
    def _(p):
        dc = (gnorm[p] - acc1[...] - ctx[p] * acc2[...]) * invb[...]
        dc = dc.astype(BF)
        dc_buf[:, lanes_of(p)] = dc
        prod = dc.astype(F32).T * ctxt[p]
        delta[p] = jnp.concatenate(
            [
                jnp.sum(prod[:HEAD_DIM], 0, keepdims=True),
                jnp.sum(prod[HEAD_DIM:], 0, keepdims=True),
            ],
            1,
        )

    each(
        sends,
        lambda side: t_copy(side).start(),
        *[lambda side, chunk=chunk: c_copy(side, chunk).start() for chunk in range(4)],
    )

    def back(p):
        key = kbuf[:, lanes_of(p)]
        val = vbuf[:, lanes_of(p)]
        dcd = diag(dc_buf[:, lanes_of(p)])
        qd = diag(qbuf[:, lanes_of(p)])
        prob = pbuf[p]
        dp = dot_nt(val, dcd)
        ds = (prob.astype(F32) * ((dp - delta[p]) * SCALE)).astype(BF)
        dkv_own[0, p] = dot_nn(ds[FR : 2 * FR], qd)
        dkv_own[1, p] = dot_nn(prob[FR : 2 * FR], dcd)
        dq_buf[:, lanes_of(p)] = pick(dot_nn(key.T, ds)).T.astype(BF)

    def back_near(p):
        key = kbuf[pl.ds(FR, FR), lanes_of(p)]
        val = vbuf[pl.ds(FR, FR), lanes_of(p)]
        qd = jnp.concatenate([diag(q_n[side, :, lanes_of(p)]) for side in range(2)], 0)
        dcd = jnp.concatenate([diag(dc_n[side, :, lanes_of(p)]) for side in range(2)], 0)
        shift = jnp.concatenate([lse_n[side, p] for side in range(2)], 1)
        dlt = jnp.concatenate([delta_n[side, p] for side in range(2)], 1)
        mask = jnp.concatenate([maskn[0], maskn[0], maskn[1], maskn[1]], 1)
        prob = jnp.exp2(dot_nt(key, qd) * (SCALE * LOG2E) + (mask - shift))
        ds = (prob * ((dot_nt(val, dcd) - dlt) * SCALE)).astype(BF)
        dk = dkv_own[0, p] + dot_nn(ds, qd)
        dv = dkv_own[1, p] + dot_nn(prob.astype(BF), dcd)
        kbuf[pl.ds(FR, FR), lanes_of(p)] = dk.astype(BF)
        vbuf[pl.ds(FR, FR), lanes_of(p)] = dv.astype(BF)

    pl.loop(0, 7)(back)

    for k in far_z:
        z_copy(za_in, 0, k).wait_recv()
    for k in far_y:
        y_copy(yb_in, 0, k).wait_recv()
    ya_in[row] = add_up(za_in, nz).astype(BF)
    zb_in[mz] = add_up(yb_in, ny).astype(BF)
    for k in far_y:
        y_copy(ya_in, 1, k).start()
    for k in far_z:
        z_copy(zb_in, 1, k).start()

    pl.loop(7, PAIRS)(back)

    dq_done = pltpu.make_async_copy(dq_buf, dq_hbm, osem.at[1])
    dq_done.start()

    each(
        takes,
        lambda side: l_copy(side).wait_recv(),
        lambda side: q_copy(side).wait_recv(),
        lambda side: t_copy(side).wait_recv(),
        lambda side: c_copy(side, 0).wait_recv(),
        lambda side: c_copy(side, 1).wait_recv(),
    )
    pl.loop(0, 5)(back_near)

    for k in far_y:
        y_copy(ya_in, 1, k).wait_recv()
    for k in far_z:
        z_copy(zb_in, 1, k).wait_recv()
    sums[pl.ds(mg * PIECE, PART)] = add_up(ya_in, ny).astype(BF)
    sums[pl.ds(mg * PIECE + PART, PART)] = add_up(zb_in, nz).astype(BF)
    for k in far_g:
        a_copy(k).start()

    each(
        takes,
        lambda side: c_copy(side, 2).wait_recv(),
        lambda side: c_copy(side, 3).wait_recv(),
    )
    pl.loop(5, PAIRS)(back_near)

    dk_done = pltpu.make_async_copy(kbuf.at[own, :], dk_hbm, osem.at[2])
    dv_done = pltpu.make_async_copy(vbuf.at[own, :], dv_hbm, osem.at[3])
    dk_done.start()
    dv_done.start()

    for k in far_g:
        a_copy(k).wait_recv()
    sums_done = pltpu.make_async_copy(sums, sums_hbm, osem.at[4])
    sums_done.start()

    def sent(buf, sem):
        remote(buf, buf, sem, sem, sides[0]).wait_send()

    each(
        sends,
        lambda side: sent(pbuf.at[pl.ds(0, 4)], kv_s.at[side]),
        lambda side: sent(dc_buf, c_s.at[side]),
        lambda side: x_copy(side).wait_send(),
        lambda side: g_copy(side).wait_send(),
        lambda side: l_copy(side).wait_send(),
        lambda side: q_copy(side).wait_send(),
        lambda side: t_copy(side).wait_send(),
    )
    others = pl.ds(0, GROUP - 1)
    sent(r_in.at[others], r_s)
    sent(r_in.at[others], a_s)
    for j in range(2):
        sent(za_in.at[pl.ds(0, nz - 1)], z_s.at[j])
        sent(yb_in.at[pl.ds(0, ny - 1)], y_s.at[j])
    sums_done.wait()
    conv_done.wait()
    dq_done.wait()
    dk_done.wait()
    dv_done.wait()


def finish(
    factor,
    conv_in,
    dq_in,
    dk_in,
    dv_in,
    sums_in,
    gain_hbm,
    ker_hbm,
    conv_out,
    dq_out,
    dk_out,
    dv_out,
    gain_out,
    ker_out,
    bias_out,
    gain_ref,
    ker_ref,
    sem,
):
    loads = [
        pltpu.make_async_copy(gain_hbm, gain_ref, sem.at[4]),
        pltpu.make_async_copy(ker_hbm, ker_ref, sem.at[5]),
    ]
    for copy in loads:
        copy.start()
    copies = [
        pltpu.make_async_copy(a, b, sem.at[i])
        for i, (a, b) in enumerate(
            ((conv_in, conv_out), (dq_in, dq_out), (dk_in, dk_out), (dv_in, dv_out))
        )
    ]
    for copy in copies:
        copy.start()
    for copy in loads:
        copy.wait()
    for c in range(PAIRS):
        at = slice(c * LANES, (c + 1) * LANES)
        gsum = jnp.zeros((8, LANES), F32)
        for rg in range(4):
            tile = sums_in[rg * PAIRS + c].astype(F32) * factor
            if rg < 3:
                ker_out[rg * 8 : rg * 8 + 8, at] = tile
                gsum = gsum + tile * ker_ref[rg * 8 : rg * 8 + 8, at]
            else:
                ker_out[24:31, at] = tile[:7]
                bias_out[at] = tile[7]
                gsum = gsum + jnp.concatenate(
                    [tile[:7] * ker_ref[24:31, at], jnp.zeros((1, LANES), F32)], 0
                )
        gain_out[at] = jnp.sum(gsum, 0) / gain_ref[at]
    for copy in copies:
        copy.wait()


def per_device(nz, ny, queries, keys, values, segment_ids, norm_gain, conv_kernel, conv_bias, cot):
    dma = pltpu.SemaphoreType.DMA
    vmem = pltpu.VMEM
    any_ = pl.BlockSpec(memory_space=pl.ANY)
    whole = pl.BlockSpec(memory_space=pltpu.VMEM)
    row = jax.ShapeDtypeStruct((FR, WIDTH), BF)
    in_hbm = functools.partial(pltpu.with_memory_space_constraint, memory_space=pltpu.HBM)
    rows = [in_hbm(a[0]) for a in (queries, keys, values, cot)]
    segment_ids, gain_in, ker_in, bias_in = map(
        in_hbm, (segment_ids, norm_gain, conv_kernel, conv_bias)
    )
    outs = pl.pallas_call(
        functools.partial(kernel, nz, ny),
        out_shape=(
            row,
            row,
            row,
            row,
            jax.ShapeDtypeStruct((TILES, 8, LANES), BF),
        ),
        in_specs=[any_] * 8,
        out_specs=(any_,) * 5,
        scratch_shapes=[
            vmem((WIDTH,), F32),
            vmem((TAPS, WIDTH), F32),
            vmem((WIDTH,), F32),
            vmem((WIDE, WIDTH), BF),
            vmem((WIDE, WIDTH), BF),
            vmem((FR, WIDTH), BF),
            vmem((FR, WIDTH), BF),
            vmem((3, 1, FR), jnp.int32),
            vmem((WIDE, LANES), jnp.int32),
            vmem((WIDE, LANES), F32),
            vmem((TAPS, FR, LANES), F32),
            vmem((PAIRS, TAPS, 8, LANES), F32),
            vmem((PAIRS, 8, LANES), F32),
            vmem((PAIRS, 8, LANES), F32),
            vmem((PAIRS, WIDE, 2 * LANES), BF),
            vmem((PAIRS, FR, LANES), F32),
            vmem((PAIRS, FR, LANES), F32),
            vmem((PAIRS, FR + 32, LANES), F32),
            vmem((PAIRS, FR + 32, LANES), F32),
            vmem((FR, LANES), F32),
            vmem((FR, LANES), F32),
            vmem((FR, LANES), F32),
            vmem((FR, LANES), F32),
            vmem((2, PAIRS, 16, LANES), BF),
            vmem((2, PAIRS, 16, LANES), BF),
            vmem((2, PAIRS, 16, LANES), BF),
            vmem((2, PAIRS, 16, LANES), BF),
            vmem((PAIRS, 32, 8, LANES), F32),
            vmem((TAPS, 8, 8, LANES), F32),
            vmem((2, PAIRS, FR, LANES), F32),
            vmem((PAIRS, FR, LANES), F32),
            vmem((2, FR, LANES), F32),
            vmem((PAIRS, 1, 2 * LANES), F32),
            vmem((2, PAIRS, 1, 2 * LANES), F32),
            vmem((PAIRS, 1, 2 * LANES), F32),
            vmem((2, PAIRS, 1, 2 * LANES), F32),
            vmem((2, FR, WIDTH), BF),
            vmem((FR, WIDTH), BF),
            vmem((2, FR, WIDTH), BF),
            vmem((FR, WIDTH), BF),
            vmem((FR, WIDTH), BF),
            vmem((TILES, 8, LANES), BF),
            vmem((GROUP, PIECE, 8, LANES), BF),
            vmem((nz, PART, 8, LANES), BF),
            vmem((ny, PART, 8, LANES), BF),
            vmem((ny, PART, 8, LANES), BF),
            vmem((nz, PART, 8, LANES), BF),
            vmem((TILES, 8, LANES), BF),
            dma((10,)),
            dma((5,)),
            dma((2,)),
            dma((2, 2, PAIRS)),
            dma((2,)),
            dma((2,)),
            dma((2,)),
            dma((2,)),
            dma((2,)),
            dma((2,)),
            dma((2,)),
            dma((2,)),
            dma((2,)),
            dma((2,)),
            dma((2,)),
            dma((2, 4)),
            dma,
            dma((GROUP - 1,)),
            dma((2,)),
            dma((2, nz - 1)),
            dma((2,)),
            dma((2, ny - 1)),
            dma,
            dma((GROUP - 1,)),
        ],
        compiler_params=pltpu.CompilerParams(
            collective_id=0, has_side_effects=True, vmem_limit_bytes=36 * 1024 * 1024
        ),
    )(
        *rows,
        segment_ids,
        gain_in,
        ker_in,
        bias_in,
    )
    factor = (ny * nz * GROUP * FR) ** (-0.5)
    vec = jax.ShapeDtypeStruct((WIDTH,), F32)
    conv_out, dq, dk, dv, gain, ker, bias = pl.pallas_call(
        functools.partial(finish, factor),
        out_shape=(row, row, row, row, vec, jax.ShapeDtypeStruct((TAPS, WIDTH), F32), vec),
        in_specs=[any_] * 4 + [whole] + [any_] * 2,
        out_specs=(any_,) * 4 + (whole,) * 3,
        scratch_shapes=[vmem((WIDTH,), F32), vmem((TAPS, WIDTH), F32), dma((6,))],
        compiler_params=pltpu.CompilerParams(vmem_limit_bytes=4 * 1024 * 1024),
    )(*outs, gain_in, ker_in)
    return (conv_out[None], dq[None], dk[None], dv[None], gain, ker, bias)


def solution(mesh):
    rows = P("dp", "seq", None)
    nz = mesh.shape["seq"] // (NX * NC)
    return jax.shard_map(
        functools.partial(per_device, nz, mesh.shape["dp"]),
        mesh=mesh,
        in_specs=(rows, rows, rows, P("dp", None), P(), P(), P(), rows),
        out_specs=(rows, rows, rows, rows, P(), P(), P()),
        check_vma=False,
    )
```
